32 devices in a mesh: gx: 4 (over z), gy: 8 (over y, x, core).
Axes of the slice: x: 2, y: 2, z: 4, core: 2. Of those that a mesh axis runs over, the one named last changes fastest.
Arguments:
- coeffs: bfloat16 [8, 64, 256, 128], P('gx', 'gy'), may hold values from -0.25 to 0.25
- permit: float32 [8, 64, 256], P('gx', 'gy'), may hold values from 0.25 to 4
- shift_diag: float32 [8, 64, 128], P('gx', 'gy'), may hold values from 0.5 to 4
- codes: int32 [8, 64, 6], P('gx', 'gy'), may hold values from 0 to 8
- counts: int32 [8, 64], P('gx', 'gy'), may hold values from 1 to 6
- weights: float32 [8, 64, 6], P('gx', 'gy'), may hold values from 0.5 to 1.5
- vectors: bfloat16 [8, 64, 128, 128], P('gx', 'gy'), may hold values from -6 to 6
Outputs:
- factor: bfloat16 [8, 64, 128, 128], P('gx', 'gy')
- applied: bfloat16 [8, 64, 128, 128], P('gx', 'gy')
The draws below stay inside these ranges and needn't reach their ends.
Inputs may be any that keep to these rules, and one draw needn't show every extreme that they name: codes name one of the 3 x 3 blocks around a block, as in the reference program.
All inputs are finite; a program needn't handle non-finite values.
Results may differ from the reference program's by a relative error of at most 0.0051.
Values may be sent and summed in bfloat16 or wider, within the bound.
A program may use at most 64 MiB of HBM per device.

```python
import math
import jax
import jax.numpy as jnp
from jax import lax

B = 128
R = 256
NV = 128
PAT = 6
BX = 8
BY = 64


def draw_coeffs(key, part):
    key_cols = jax.random.fold_in(key, 11)
    key_rows = jax.random.fold_in(key, 23)
    column_noise = jax.random.normal(key_cols, (BX, BY, R, B + 1), jnp.float32)
    row_common = jax.random.normal(key_rows, (BX, BY, R, 1), jnp.float32)
    mixed = column_noise[:, :, :, 1:] + 0.9 * column_noise[:, :, :, :-1] + 1.5 * row_common
    values = mixed * jnp.float32(0.031)
    values = jnp.clip(values, -0.25, 0.25)
    return values.astype(jnp.bfloat16)


def touch_ends(values, key, low, largest):
    shape = values.shape
    place = [jax.random.randint(jax.random.fold_in(key, axis), (), 0, shape[axis]) for axis in range(len(shape))]
    values = values.at[tuple(place)].set(low)
    longest = shape.index(max(shape))
    place[longest] = (place[longest] + 1) % shape[longest]
    return values.at[tuple(place)].set(largest)


def steps_of(rng, dims, cuts, low, high):
    def one(dim, blocks):
        heights = jax.random.uniform(jax.random.fold_in(jax.random.fold_in(rng, 6), dim), (blocks,), jnp.float32, low / len(cuts), high / len(cuts))
        return jnp.repeat(jnp.exp(heights), dims[dim] // blocks).reshape((-1,) + (1,) * (len(dims) - dim - 1))

    gain = one(*cuts[0])
    for cut in cuts[1:]:
        gain = gain * one(*cut)
    return gain


def noise(own_key, shape, spread, reach, cuts=(), kind=jnp.bfloat16):
    drawn = jax.random.normal(own_key, shape, jnp.float32) * spread
    if len(cuts) > 0:
        drawn = steps_of(own_key, shape, cuts, -0.22, 0.18) * drawn
    return jnp.clip(drawn, min=-reach, max=reach).astype(kind)


def setup_inputs(seed: int = 0) -> dict:
    keys = jax.random.split(jax.random.key(seed), 8)
    coeffs = draw_coeffs(jax.random.fold_in(keys[7], 71), 0)
    permit = jnp.clip(jnp.exp(math.log(4.0) - 2.7725887 * jax.random.uniform(keys[1], (BX, BY, R), jnp.float32) ** steps_of(keys[1], (BX, BY, R), ((0, 4), (1, 8)), -0.2, 0.2)), 0.25, 4.0)
    shift_diag = jnp.clip(jnp.exp(math.log(4.0) - 2.0794415 * jax.random.uniform(keys[2], (BX, BY, B), jnp.float32) ** steps_of(keys[2], (BX, BY, B), ((0, 4), (1, 8)), -0.2, 0.2)), 0.5, 4.0)
    codes = touch_ends(jax.random.randint(keys[3], (BX, BY, PAT), 0, 9), jax.random.fold_in(keys[3], 1), 0, 8).astype(jnp.int32)
    counts = touch_ends(jax.random.randint(keys[4], (BX, BY), 1, PAT + 1), jax.random.fold_in(keys[4], 1), 1, PAT).astype(jnp.int32)
    weights = jnp.clip(0.5 + 1.0 * jax.random.uniform(keys[5], (BX, BY, PAT), jnp.float32) ** steps_of(keys[5], (BX, BY, PAT), ((0, 4), (1, 8)), -0.2, 0.2), 0.5, 1.5)
    vectors = noise(keys[6], (BX, BY, B, NV), 1.0, 6.0, ((0, 4), (1, 8)))
    return dict(coeffs=coeffs, permit=permit, shift_diag=shift_diag, codes=codes, counts=counts, weights=weights, vectors=vectors)


def reference(coeffs, permit, shift_diag, codes, counts, weights, vectors):
    padded = jnp.pad(coeffs, ((1, 1), (1, 1), (0, 0), (0, 0)))
    columns = jnp.arange(BY)

    def block_row(row_at):
        window = lax.dynamic_slice_in_dim(padded, row_at, 3, 0)
        permit_row = permit[row_at]
        code_row = codes[row_at]
        count_row = counts[row_at]
        gram = jnp.zeros((BY, B, B), jnp.float32)
        for slot_num in range(PAT):
            slot_code = code_row[:, slot_num]
            neighbour = window[slot_code // 3, columns + slot_code % 3]
            scaled = (permit_row[:, :, None] * neighbour.astype(jnp.float32)).astype(jnp.bfloat16)
            product = jnp.einsum('yrk,yrl->ykl', scaled.astype(jnp.float32), neighbour.astype(jnp.float32))
            gram = gram + jnp.where((slot_num < count_row)[:, None, None], product, jnp.float32(0.0))
        system = gram + shift_diag[row_at][:, :, None] * jnp.eye(B, dtype=jnp.float32)
        cholesky_factor = jnp.linalg.cholesky(system)
        identity = jnp.broadcast_to(jnp.eye(B, dtype=system.dtype), system.shape)
        inverse = lax.linalg.triangular_solve(cholesky_factor, identity, left_side=True, lower=True)
        factor_row = inverse.astype(jnp.bfloat16)
        images = jnp.einsum('ykl,ykv->ylv', factor_row.astype(jnp.float32), vectors[row_at].astype(jnp.float32))
        return (factor_row, images)
    factor, images = lax.map(block_row, jnp.arange(BX))
    active = jnp.arange(PAT)[None, None, :] < counts[:, :, None]
    gathered_sum = jnp.zeros((BX + 2, BY + 2, B, NV), jnp.float32)
    for offset in range(9):
        weight_sum = jnp.sum(jnp.where(active & (codes == offset), weights, jnp.float32(0.0)), axis=-1)
        gathered_sum = gathered_sum.at[offset // 3:offset // 3 + BX, offset % 3:offset % 3 + BY].add(weight_sum[:, :, None, None] * images)
    applied = gathered_sum[1:-1, 1:-1].astype(jnp.bfloat16)
    return (factor, applied)
```

```python
import functools

import jax
import jax.numpy as jnp
from jax import lax
from jax.experimental import pallas as pl
from jax.experimental.pallas import tpu as pltpu
from jax.sharding import PartitionSpec as P

MESH = pl.DeviceIdType.MESH
BASE = 32
WIDTH = 4
DIRS = ((1, 0), (-1, 0), (0, 1), (0, -1), (1, 1), (1, -1), (-1, 1), (-1, -1))


def neighbours():
    sizes = (lax.axis_size("gx"), lax.axis_size("gy"))
    me = (lax.axis_index("gx"), lax.axis_index("gy"))

    def there(d):
        return (me[0] + d[0], me[1] + d[1])

    def exists(d):
        ok = None
        for size, at, step in zip(sizes, me, d):
            if step == 0:
                continue
            test = (at + 1 < size) if step > 0 else (at > 0)
            ok = test if ok is None else jnp.logical_and(ok, test)
        return ok

    return there, exists


def gram_kernel(c_ref, permit_ref, shift_ref, codes_ref, counts_ref, weights_ref, gram_ref, wt, cs, ts, own_sem, send_sem, recv_sem):
    bx, by, coupling, order = c_ref.shape
    slots = codes_ref.shape[0]
    wide = by + 2
    there, exists = neighbours()
    row = {1: bx - 1, -1: 0}
    col = {1: by - 1, -1: 0}
    land_row = {1: 0, -1: bx + 1}
    land_col = {1: 0, -1: by + 1}
    gx_dirs, gy_dirs, corners = DIRS[:2], DIRS[2:4], DIRS[4:]
    own = [pltpu.make_async_copy(c_ref.at[x], cs.at[pl.ds((x + 1) * wide + 1, by)], own_sem.at[x]) for x in range(bx)]
    for copy in own:
        copy.start()
    barrier = pltpu.get_barrier_semaphore()
    for d in DIRS:
        @pl.when(exists(d))
        def _(d=d):
            pl.semaphore_signal(barrier, inc=1, device_id=there(d), device_id_type=MESH)
    near = [exists(d).astype(jnp.int32) for d in DIRS[:4]]
    pl.semaphore_wait(barrier, (near[0] + near[1] + 1) * (near[2] + near[3] + 1) - 1)

    def remote(source, target, k, d):
        return pltpu.make_async_remote_copy(
            src_ref=source, dst_ref=cs.at[target], send_sem=send_sem.at[k], recv_sem=recv_sem.at[k],
            device_id=there(d), device_id_type=MESH)

    def gy_copy(j, x):
        d = gy_dirs[j]
        return remote(c_ref.at[x, col[d[1]]], (x + 1) * wide + land_col[d[1]], 4 + j * bx + x, d)

    def corner_copy(j):
        d = corners[j]
        return remote(c_ref.at[row[d[0]], col[d[1]]], land_row[d[0]] * wide + land_col[d[1]], j, d)

    def gx_copy(j, y):
        d = gx_dirs[j]
        return remote(c_ref.at[row[d[0]], y], land_row[d[0]] * wide + y + 1, 4 + 2 * bx + 2 * y + j, d)

    for j, d in enumerate(corners):
        @pl.when(exists(d))
        def _(j=j):
            corner_copy(j).start()
    for j, d in enumerate(gx_dirs):
        @pl.when(exists(d))
        def _(j=j):
            for y in range(by):
                gx_copy(j, y).start()
    for j, d in enumerate(gy_dirs):
        @pl.when(exists(d))
        def _(j=j):
            for x in range(bx):
                gy_copy(j, x).start()

    zero = jnp.zeros((coupling, order), cs.dtype)
    for j, d in enumerate(corners):
        @pl.when(jnp.logical_not(exists((-d[0], -d[1]))))
        def _(d=d):
            cs[land_row[d[0]] * wide + land_col[d[1]]] = zero
    for j, d in enumerate(gx_dirs):
        @pl.when(jnp.logical_not(exists((-d[0], -d[1]))))
        def _(d=d):
            @pl.loop(0, by)
            def _(y):
                cs[land_row[d[0]] * wide + y + 1] = zero
    for j, d in enumerate(gy_dirs):
        @pl.when(jnp.logical_not(exists((-d[0], -d[1]))))
        def _(d=d):
            for x in range(bx):
                cs[(x + 1) * wide + land_col[d[1]]] = zero

    def turn(n):
        ts[n] = cs[n].T

    def terms(x, y, pairs):
        p = permit_ref[x, pl.ds(y, 1), :]
        acc = None
        for ax, ay in pairs:
            n = (x + ax) * wide + y + ay
            times = jnp.int32(0)
            for s in range(slots):
                hit = (codes_ref[s, x, y] == ax * 3 + ay) & (s < counts_ref[x, y])
                times = times + hit.astype(jnp.int32)
            scaled = (ts[n].astype(jnp.float32) * p).astype(jnp.bfloat16)
            term = times.astype(jnp.float32) * jnp.dot(scaled, cs[n], preferred_element_type=jnp.float32)
            acc = term if acc is None else acc + term
        return acc

    inside = {x: [ax for ax in range(3) if 0 <= x + ax - 1 < bx] for x in range(bx)}
    outside = {x: [ax for ax in range(3) if not 0 <= x + ax - 1 < bx] for x in range(bx)}

    @pl.loop(0, by)
    def _(y):
        for x in range(bx):
            for offset in range(9):
                w = jnp.float32(0.0)
                for s in range(slots):
                    hit = (codes_ref[s, x, y] == offset) & (s < counts_ref[x, y])
                    w = w + jnp.where(hit, weights_ref[s, x, y], 0.0)
                wt[offset, x * by + y] = w

    for copy in own:
        copy.wait()
    for x in range(bx):
        @pl.loop(0, by)
        def _(y):
            turn((x + 1) * wide + y + 1)
    for x in range(bx):
        @pl.loop(1, by - 1)
        def _(y):
            gram_ref[x, y] = terms(x, y, [(ax, ay) for ax in inside[x] for ay in range(3)])
    for j, d in enumerate(gy_dirs):
        @pl.when(exists((-d[0], -d[1])))
        def _(j=j):
            for x in range(bx):
                gy_copy(j, x).wait_recv()
    for x in range(bx):
        turn((x + 1) * wide)
        turn((x + 1) * wide + by + 1)
    for x in range(bx):
        @pl.loop(0, 2)
        def _(e):
            y = e * (by - 1)
            gram_ref[x, y] = terms(x, y, [(ax, ay) for ax in inside[x] for ay in range(3)])

    same = lax.broadcasted_iota(jnp.int32, (order, order), 0) == lax.broadcasted_iota(jnp.int32, (order, order), 1)

    def finished(x, y, acc):
        gram_ref[x, y] = 0.5 * (acc + acc.T) + jnp.where(same, shift_ref[x, pl.ds(y, 1), :], 0.0)

    for x in range(1, bx - 1):
        @pl.loop(0, by)
        def _(y):
            finished(x, y, gram_ref[x, y])
    for j, d in enumerate(corners):
        @pl.when(exists((-d[0], -d[1])))
        def _(j=j):
            corner_copy(j).wait_recv()
    for r in (0, bx + 1):
        turn(r * wide)
        turn(r * wide + by + 1)

    def arrive(y):
        for j, d in enumerate(gx_dirs):
            @pl.when(exists((-d[0], -d[1])))
            def _(j=j):
                gx_copy(j, y).wait_recv()
        turn(y + 1)
        turn((bx + 1) * wide + y + 1)

    def last(y):
        for x in sorted({0, bx - 1}):
            finished(x, y, gram_ref[x, y] + terms(x, y, [(ax, ay) for ax in outside[x] for ay in range(3)]))

    arrive(0)

    @pl.loop(1, by)
    def _(y):
        arrive(y)
        last(y - 1)

    last(by - 1)
    for j, d in enumerate(corners):
        @pl.when(exists(d))
        def _(j=j):
            corner_copy(j).wait_send()
    for j, d in enumerate(gx_dirs):
        @pl.when(exists(d))
        def _(j=j):
            for y in range(by):
                gx_copy(j, y).wait_send()
    for j, d in enumerate(gy_dirs):
        @pl.when(exists(d))
        def _(j=j):
            for x in range(bx):
                gy_copy(j, x).wait_send()


def split(x):
    h = x.astype(jnp.bfloat16)
    return h, (x - h.astype(jnp.float32)).astype(jnp.bfloat16)


def factor_kernel(gram_ref, out_ref, fac_ref, gs, sem):
    bx, by, order = gram_ref.shape[:3]
    blocks = bx * by
    for i in range(blocks):
        gs[i] = gram_ref[i // by, i % by]
    factor(gs, fac_ref, bx, by, order)
    copy = pltpu.make_async_copy(fac_ref, out_ref, sem)
    copy.start()
    copy.wait()


def factor(gs, fac_ref, bx, by, order):
    blocks = bx * by
    lanes = lax.broadcasted_iota(jnp.int32, (order, order), 1)
    per = order // BASE
    seg = lax.broadcasted_iota(jnp.int32, (BASE, order), 1) // BASE
    place = lax.broadcasted_iota(jnp.int32, (BASE, order), 1) % BASE
    row = lax.broadcasted_iota(jnp.int32, (BASE, order), 0)
    seg8, place8, row8 = seg[:8], place[:8], row[:8]
    masks = [jnp.where(seg == q, 1.0, 0.0).astype(jnp.bfloat16) for q in range(per)]
    tops = BASE // 8
    groups = blocks // per
    for stage in range(per):
        low = stage * BASE
        high = low + BASE
        packs = []
        for g in range(groups):
            pack = None
            for q in range(per):
                piece = gs[g * per + q, low:high, :]
                shift = (q * BASE - low) % order
                piece = pltpu.roll(piece, shift, axis=1) if shift else piece
                pack = piece if pack is None else jnp.where(seg == q, piece, pack)
            packs.append([pack[8 * c:8 * c + 8] for c in range(tops)])
        pivots = [[jnp.ones((8, order), jnp.float32) for _ in range(tops)] for _ in range(groups)]
        for first in range(0, BASE, WIDTH):
            top = first // 8
            cols = [[[jnp.take_along_axis(m[c], seg8 * BASE + (first + j), axis=1) for c in range(top, tops)]
                     for j in range(WIDTH)] for m in packs]
            for j in range(WIDTH):
                k = first + j
                at = k - 8 * top
                for g, m in enumerate(packs):
                    f = cols[g][j]
                    d = jnp.broadcast_to(f[0][at:at + 1], (8, order))
                    inv_d = 1.0 / d
                    pivots[g][top] = jnp.where(row8 == at, d, pivots[g][top])
                    f = [jnp.where(row8 > at, f[0], 0.0)] + f[1:]
                    for n in range(j + 1, WIDTH):
                        t = jnp.broadcast_to(cols[g][n][0][at:at + 1], (8, order)) * inv_d
                        cols[g][n] = [x - y * t for x, y in zip(cols[g][n], f)]
                    r = (jnp.broadcast_to(m[top][at:at + 1], (8, order)) + jnp.where(place8 == k, 1.0, 0.0)) * inv_d
                    for c in range(top, tops):
                        m[c] = m[c] - f[c - top] * r
        for g, m in enumerate(packs):
            m = jnp.concatenate(m, axis=0)
            unit = jnp.where(row > place, m, jnp.where(row == place, 1.0, 0.0))
            inv = unit * lax.rsqrt(jnp.concatenate(pivots[g], axis=0))
            inv_h, inv_l = split(inv)
            wide_h = jnp.concatenate([inv_h * mask for mask in masks], axis=0)
            wide_l = jnp.concatenate([inv_l * mask for mask in masks], axis=0)
            panel = []
            for q in range(per):
                here = gs[g * per + q, low:high, :]
                panel.append(jnp.where(seg == stage, jnp.where(row == place, 1.0, 0.0), here))
            panel_h, panel_l = split(jnp.concatenate(panel, axis=0))
            whole = jnp.dot(jnp.concatenate([wide_h, wide_h, wide_l], axis=1),
                            jnp.concatenate([panel_h, panel_l, panel_h], axis=0),
                            preferred_element_type=jnp.float32)
            for q in range(per):
                at = g * per + q
                part = whole[q * BASE:(q + 1) * BASE]
                fac_ref[at // by, at % by, low:high, :] = jnp.where(seg <= stage, part, 0.0).astype(fac_ref.dtype)
                if high < order:
                    h, l = split(part)
                    left = jnp.concatenate([h, h, l], axis=0).T
                    update = jnp.dot(left[high:], jnp.concatenate([h, l, h], axis=0), preferred_element_type=jnp.float32)
                    below = gs[at, high:, :]
                    below = jnp.where(lanes[high:] // BASE == stage, 0.0, below)
                    gs[at, high:, :] = below - update


def sum_kernel(fac_ref, v_ref, wt, out_ref, img, loc, px, py, pc, rx, ry, rc, send_sem, recv_sem):
    bx, by = fac_ref.shape[:2]
    there, exists = neighbours()
    sends = [px.at[0], px.at[1], py.at[0], py.at[1]] + [pc.at[k] for k in range(4)]
    lands = [rx.at[0], rx.at[1], ry.at[0], ry.at[1]] + [rc.at[k] for k in range(4)]
    barrier = pltpu.get_barrier_semaphore()
    for d in DIRS:
        @pl.when(exists(d))
        def _(d=d):
            pl.semaphore_signal(barrier, inc=1, device_id=there(d), device_id_type=MESH)
    for k, d in enumerate(DIRS):
        @pl.when(jnp.logical_not(exists((-d[0], -d[1]))))
        def _(k=k):
            lands[k][...] = jnp.zeros(lands[k].shape, lands[k].dtype)

    @pl.loop(0, by)
    def _(y):
        for x in range(bx):
            img[x, y] = lax.dot_general(fac_ref[x, y], v_ref[x, y], (((0,), (0,)), ((), ())),
                                        preferred_element_type=jnp.float32)

    def target(tx, ty):
        total = None
        for x in range(bx):
            for y in range(by):
                ax, ay = tx - x, ty - y
                if 0 <= ax < 3 and 0 <= ay < 3:
                    term = wt[ax * 3 + ay, x * by + y] * img[x, y]
                    total = term if total is None else total + term
        return total

    for y in range(by):
        px[0, y] = target(bx + 1, y + 1).astype(px.dtype)
        px[1, y] = target(0, y + 1).astype(px.dtype)
    for k, d in enumerate(DIRS[4:]):
        pc[k] = target(bx + 1 if d[0] > 0 else 0, by + 1 if d[1] > 0 else 0).astype(pc.dtype)
    for x in range(bx):
        py[0, x] = target(x + 1, by + 1).astype(py.dtype)
        py[1, x] = target(x + 1, 0).astype(py.dtype)
    near = [exists(d).astype(jnp.int32) for d in DIRS[:4]]
    pl.semaphore_wait(barrier, (near[0] + near[1] + 1) * (near[2] + near[3] + 1) - 1)

    def copy(k, d):
        return pltpu.make_async_remote_copy(
            src_ref=sends[k], dst_ref=lands[k], send_sem=send_sem.at[k], recv_sem=recv_sem.at[k],
            device_id=there(d), device_id_type=MESH)

    order_of = (4, 5, 6, 7, 0, 1, 2, 3)
    for k in order_of:
        @pl.when(exists(DIRS[k]))
        def _(k=k):
            copy(k, DIRS[k]).start()
    for x in range(bx):
        for y in range(by):
            loc[x, y] = target(x + 1, y + 1)
    for k in order_of:
        @pl.when(exists((-DIRS[k][0], -DIRS[k][1])))
        def _(k=k):
            copy(k, DIRS[k]).wait_recv()
    for x in range(bx):
        for y in range(by):
            total = loc[x, y]
            for k, edge in ((0, 0), (1, bx - 1)):
                if x == edge:
                    total = total + rx[k, y].astype(jnp.float32)
            for k, edge in ((0, 0), (1, by - 1)):
                if y == edge:
                    total = total + ry[k, x].astype(jnp.float32)
            for k, place in enumerate(((0, 0), (0, by - 1), (bx - 1, 0), (bx - 1, by - 1))):
                if (x, y) == place:
                    total = total + rc[k].astype(jnp.float32)
            out_ref[x, y] = total.astype(out_ref.dtype)
    for k in order_of:
        @pl.when(exists(DIRS[k]))
        def _(k=k):
            copy(k, DIRS[k]).wait_send()


def local(coeffs, permit, shift_diag, codes, counts, weights, vectors):
    bx, by, coupling, order = coeffs.shape
    nv = vectors.shape[3]
    bf16, f32 = jnp.bfloat16, jnp.float32
    anyspace = pl.BlockSpec(memory_space=pl.ANY)
    vmem = pl.BlockSpec(memory_space=pltpu.VMEM)
    smem = pl.BlockSpec(memory_space=pltpu.SMEM)
    codes, weights = jnp.transpose(codes, (2, 0, 1)), jnp.transpose(weights, (2, 0, 1))
    padded = (bx + 2) * (by + 2)
    copies = 4 + 2 * bx + 2 * by
    gram, sums = pl.pallas_call(
        gram_kernel,
        out_shape=(pltpu.VMEM((bx, by, order, order), f32), jax.ShapeDtypeStruct((9, bx * by), f32)),
        in_specs=[anyspace, vmem, vmem, smem, smem, smem],
        out_specs=(vmem, smem),
        scratch_shapes=[
            pltpu.VMEM((padded, coupling, order), bf16),
            pltpu.VMEM((padded, order, coupling), bf16),
            pltpu.SemaphoreType.DMA((bx,)),
            pltpu.SemaphoreType.DMA((copies,)), pltpu.SemaphoreType.DMA((copies,)),
        ],
        compiler_params=pltpu.CompilerParams(collective_id=0, has_side_effects=True),
        name="gram",
    )(coeffs, permit, shift_diag, codes, counts, weights)
    fac, held = pl.pallas_call(
        factor_kernel,
        out_shape=(jax.ShapeDtypeStruct((bx, by, order, order), bf16), pltpu.VMEM((bx, by, order, order), bf16)),
        in_specs=[vmem],
        out_specs=(anyspace, vmem),
        scratch_shapes=[pltpu.VMEM((bx * by, order, order), f32), pltpu.SemaphoreType.DMA],
        name="factor",
    )(pltpu.with_memory_space_constraint(gram, pltpu.VMEM))
    edges = [
        pltpu.VMEM((2, by, order, nv), bf16),
        pltpu.VMEM((2, bx, order, nv), bf16),
        pltpu.VMEM((4, order, nv), bf16),
    ]
    applied = pl.pallas_call(
        sum_kernel,
        out_shape=pltpu.VMEM((bx, by, order, nv), bf16),
        in_specs=[vmem, vmem, smem],
        out_specs=vmem,
        scratch_shapes=[
            pltpu.VMEM((bx, by, order, nv), f32),
            pltpu.VMEM((bx, by, order, nv), f32),
            *edges, *edges,
            pltpu.SemaphoreType.DMA((8,)), pltpu.SemaphoreType.DMA((8,)),
        ],
        compiler_params=pltpu.CompilerParams(collective_id=1, has_side_effects=True),
        name="sums",
    )(pltpu.with_memory_space_constraint(held, pltpu.VMEM), vectors, sums)
    return fac, applied


def solution(mesh):
    placed = (
        P("gx", "gy", None, None),
        P("gx", "gy", None),
        P("gx", "gy", None),
        P("gx", "gy", None),
        P("gx", "gy"),
        P("gx", "gy", None),
        P("gx", "gy", None, None),
    )
    return jax.shard_map(
        local,
        mesh=mesh,
        in_specs=placed,
        out_specs=(P("gx", "gy", None, None), P("gx", "gy", None, None)),
        check_vma=False,
    )
```

```python
import functools

import jax
import jax.numpy as jnp
from jax import lax
from jax.experimental import pallas as pl
from jax.experimental.pallas import tpu as pltpu
from jax.sharding import PartitionSpec as P

MESH = pl.DeviceIdType.MESH
BASE = 32
WIDTH = 4
DIRS = ((1, 0), (-1, 0), (0, 1), (0, -1), (1, 1), (1, -1), (-1, 1), (-1, -1))


def neighbours():
    sizes = (lax.axis_size("gx"), lax.axis_size("gy"))
    me = (lax.axis_index("gx"), lax.axis_index("gy"))

    def there(d):
        return (me[0] + d[0], me[1] + d[1])

    def exists(d):
        ok = None
        for size, at, step in zip(sizes, me, d):
            if step == 0:
                continue
            test = (at + 1 < size) if step > 0 else (at > 0)
            ok = test if ok is None else jnp.logical_and(ok, test)
        return ok

    return there, exists


def gram_kernel(c_ref, permit_ref, shift_ref, codes_ref, counts_ref, weights_ref, gram_ref, wrow_ref,
                cs, ts, pm, sh, cd, ct, wg, flat, tp, tq, ps, pr, own_sem, in_sem, send_sem, recv_sem):
    bx, by, coupling, order = c_ref.shape
    slots = codes_ref.shape[0]
    wide = by + 2
    quarter = order // 4
    packed = pr.shape[2]
    there, exists = neighbours()
    edge = {1: by - 1, -1: 0}
    land = {1: 0, -1: by + 1}
    gx_dirs, gy_dirs = DIRS[:2], DIRS[2:4]
    small = [pltpu.make_async_copy(source, target, in_sem.at[k]) for k, (source, target) in enumerate((
        (codes_ref, cd), (counts_ref, ct), (weights_ref, wg), (permit_ref, pm), (shift_ref, sh)))]
    own = [pltpu.make_async_copy(c_ref.at[x], cs.at[pl.ds(x * wide + 1, by)], own_sem.at[x]) for x in range(bx)]
    barrier = pltpu.get_barrier_semaphore()
    for d in DIRS[:4]:
        @pl.when(exists(d))
        def _(d=d):
            pl.semaphore_signal(barrier, inc=1, device_id=there(d), device_id_type=MESH)
    for copy in small + own:
        copy.start()

    def remote(source, target, k, d):
        return pltpu.make_async_remote_copy(
            src_ref=source, dst_ref=target, send_sem=send_sem.at[k], recv_sem=recv_sem.at[k],
            device_id=there(d), device_id_type=MESH)

    def gy_copy(j, x):
        d = gy_dirs[j]
        return remote(c_ref.at[x, edge[d[1]]], cs.at[x * wide + land[d[1]]], j * bx + x, d)

    def scale_copy(j):
        x, o = ((bx - 1, 6), (0, 0))[j]
        return remote(tp.at[x, pl.ds(o, 3)], tq.at[j], 2 * bx + j, gx_dirs[j])

    def part_copy(j, y):
        return remote(ps.at[j, y], pr.at[j, y], 2 * bx + 2 + j * by + y, gx_dirs[1 - j])

    for copy in small[:4]:
        copy.wait()
    flat[...] = jnp.zeros(flat.shape, flat.dtype)
    half = order // 2
    for o in range(9):
        times = jnp.zeros((bx, by), jnp.float32)
        total = jnp.zeros((bx, by), jnp.float32)
        for s in range(slots):
            hit = (cd[s] == o) & (s < ct[...])
            times = times + jnp.where(hit, 1.0, 0.0)
            total = total + jnp.where(hit, wg[s], 0.0)
        flat[o * bx:(o + 1) * bx, 0:by] = times
        flat[half + o * bx:half + (o + 1) * bx, 0:by] = total
    turned = flat[...].T[0:by]

    def column(c):
        return jnp.take_along_axis(turned, jnp.full((by, order), c, jnp.int32), axis=1)

    for o in (6, 7, 8, 0, 1, 2, 3, 4, 5):
        for x in range(bx):
            times = column(o * bx + x)
            tp[x, o] = pm[x] * jnp.concatenate([times] * (coupling // order), axis=1)
            wrow_ref[o, x] = column(half + o * bx + x)

    near = [exists(d).astype(jnp.int32) for d in DIRS[:4]]
    pl.semaphore_wait(barrier, near[0] + near[1] + near[2] + near[3])
    for j, d in enumerate(gx_dirs):
        @pl.when(exists(d))
        def _(j=j):
            scale_copy(j).start()
    for j, d in enumerate(gy_dirs):
        @pl.when(exists(d))
        def _(j=j):
            for x in range(bx):
                gy_copy(j, x).start()

    zero = jnp.zeros((coupling, order), cs.dtype)
    for j, d in enumerate(gy_dirs):
        @pl.when(jnp.logical_not(exists((-d[0], -d[1]))))
        def _(d=d):
            for x in range(bx):
                cs[x * wide + land[d[1]]] = zero

    def turn(n):
        ts[n] = cs[n].T

    def terms(r, y, scales):
        left = jnp.concatenate([(ts[r * wide + y + ay].astype(jnp.float32) * scales(ay)).astype(jnp.bfloat16)
                                for ay in range(3)], axis=1)
        right = cs[pl.ds(r * wide + y, 3)].reshape(3 * coupling, order)
        return jnp.dot(left, right, preferred_element_type=jnp.float32)

    same = lax.broadcasted_iota(jnp.int32, (order, order), 0) == lax.broadcasted_iota(jnp.int32, (order, order), 1)

    def inner(y):
        for x in range(bx):
            acc = jnp.where(same, sh[x, pl.ds(y, 1), :], 0.0)
            for r in range(max(0, x - 1), min(bx, x + 2)):
                acc = acc + terms(r, y, lambda ay: tp[x, (r - x + 1) * 3 + ay, pl.ds(y, 1), :])
            gram_ref[x, y] = acc

    lane = lax.broadcasted_iota(jnp.int32, (quarter, order), 1)

    def outer(j, y):
        acc = terms((0, bx - 1)[j], y, lambda ay: tq[j, ay, pl.ds(y, 1), :])
        ps[j, y, 0:quarter] = acc[0:quarter]
        ps[j, y, quarter:2 * quarter] = jnp.where(
            lane < quarter, pltpu.roll(acc[3 * quarter:], quarter, axis=1), acc[quarter:2 * quarter])
        mid = 2 * quarter + quarter // 2
        ps[j, y, 2 * quarter:mid] = jnp.where(
            lane[:quarter // 2] < 2 * quarter, pltpu.roll(acc[mid:3 * quarter], 2 * quarter, axis=1), acc[2 * quarter:mid])

    def send(j, y):
        @pl.when(exists(gx_dirs[1 - j]))
        def _():
            part_copy(j, y).start()

    for copy in own:
        copy.wait()
    small[4].wait()
    for x in range(bx):
        @pl.loop(0, by, unroll=2)
        def _(y):
            turn(x * wide + y + 1)
    split_at = by // 2

    @pl.loop(1, split_at)
    def _(y):
        inner(y)

    for j in range(2):
        @pl.when(exists(gx_dirs[1 - j]))
        def _(j=j):
            scale_copy(j).wait_recv()
    for y in range(1, by - 1):
        for j in range(2):
            outer(j, y)
        for j in range(2):
            send(j, y)
    for j, d in enumerate(gy_dirs):
        @pl.when(exists((-d[0], -d[1])))
        def _(j=j):
            for x in range(bx):
                gy_copy(j, x).wait_recv()
    for x in range(bx):
        turn(x * wide)
        turn(x * wide + by + 1)
    for y in sorted({0, by - 1}):
        for j in range(2):
            outer(j, y)
        for j in range(2):
            send(j, y)

    @pl.loop(split_at, by - 1)
    def _(y):
        inner(y)

    @pl.loop(0, 2)
    def _(e):
        inner(e * (by - 1))

    mid = 2 * quarter + quarter // 2
    for y in list(range(1, by - 1)) + sorted({0, by - 1}):
        for j in range(2):
            @pl.when(exists(gx_dirs[j]))
            def _(j=j, y=y):
                part_copy(j, y).wait_recv()
                x = (bx - 1, 0)[j]
                gram_ref[x, y, 0:quarter] += pr[j, y, 0:quarter]
                both = pr[j, y, quarter:2 * quarter]
                gram_ref[x, y, quarter:2 * quarter] += both
                gram_ref[x, y, 3 * quarter:] += pltpu.roll(both, 3 * quarter, axis=1)
                both = pr[j, y, 2 * quarter:mid]
                gram_ref[x, y, 2 * quarter:mid] += both
                gram_ref[x, y, mid:3 * quarter] += pltpu.roll(both, 2 * quarter, axis=1)
    for j in range(2):
        @pl.when(exists(gx_dirs[j]))
        def _(j=j):
            scale_copy(j).wait_send()

        @pl.when(exists(gx_dirs[1 - j]))
        def _(j=j):
            for y in range(by):
                part_copy(j, y).wait_send()

        @pl.when(exists(gy_dirs[j]))
        def _(j=j):
            for x in range(bx):
                gy_copy(j, x).wait_send()


def split(x):
    h = x.astype(jnp.bfloat16)
    return h, (x - h.astype(jnp.float32)).astype(jnp.bfloat16)


def factor_kernel(gram_ref, out_ref, fac_ref, gs, sem):
    bx, by, order = gram_ref.shape[:3]
    blocks = bx * by
    for i in range(blocks):
        gs[i] = gram_ref[i // by, i % by]
    factor(gs, fac_ref, bx, by, order)
    copy = pltpu.make_async_copy(fac_ref, out_ref, sem)
    copy.start()
    copy.wait()


def factor(gs, fac_ref, bx, by, order):
    blocks = bx * by
    lanes = lax.broadcasted_iota(jnp.int32, (order, order), 1)
    per = order // BASE
    seg = lax.broadcasted_iota(jnp.int32, (BASE, order), 1) // BASE
    place = lax.broadcasted_iota(jnp.int32, (BASE, order), 1) % BASE
    row = lax.broadcasted_iota(jnp.int32, (BASE, order), 0)
    seg8, place8, row8 = seg[:8], place[:8], row[:8]
    masks = [jnp.where(seg == q, 1.0, 0.0).astype(jnp.bfloat16) for q in range(per)]
    tops = BASE // 8
    groups = blocks // per
    for stage in range(per):
        low = stage * BASE
        high = low + BASE
        packs = []
        for g in range(groups):
            pack = None
            for q in range(per):
                piece = gs[g * per + q, low:high, :]
                shift = (q * BASE - low) % order
                piece = pltpu.roll(piece, shift, axis=1) if shift else piece
                pack = piece if pack is None else jnp.where(seg == q, piece, pack)
            packs.append([pack[8 * c:8 * c + 8] for c in range(tops)])
        pivots = [[jnp.ones((8, order), jnp.float32) for _ in range(tops)] for _ in range(groups)]
        for first in range(0, BASE, WIDTH):
            top = first // 8
            cols = [[[jnp.take_along_axis(m[c], seg8 * BASE + (first + j), axis=1) for c in range(top, tops)]
                     for j in range(WIDTH)] for m in packs]
            for j in range(WIDTH):
                k = first + j
                at = k - 8 * top
                for g, m in enumerate(packs):
                    f = cols[g][j]
                    d = jnp.broadcast_to(f[0][at:at + 1], (8, order))
                    inv_d = 1.0 / d
                    pivots[g][top] = jnp.where(row8 == at, d, pivots[g][top])
                    f = [jnp.where(row8 > at, f[0], 0.0)] + f[1:]
                    for n in range(j + 1, WIDTH):
                        t = jnp.broadcast_to(cols[g][n][0][at:at + 1], (8, order)) * inv_d
                        cols[g][n] = [x - y * t for x, y in zip(cols[g][n], f)]
                    r = (jnp.broadcast_to(m[top][at:at + 1], (8, order)) + jnp.where(place8 == k, 1.0, 0.0)) * inv_d
                    for c in range(top, tops):
                        m[c] = m[c] - f[c - top] * r
        for g, m in enumerate(packs):
            m = jnp.concatenate(m, axis=0)
            unit = jnp.where(row > place, m, jnp.where(row == place, 1.0, 0.0))
            inv = unit * lax.rsqrt(jnp.concatenate(pivots[g], axis=0))
            inv_h, inv_l = split(inv)
            wide_h = jnp.concatenate([inv_h * mask for mask in masks], axis=0)
            wide_l = jnp.concatenate([inv_l * mask for mask in masks], axis=0)
            panel = []
            for q in range(per):
                here = gs[g * per + q, low:high, :]
                panel.append(jnp.where(seg == stage, jnp.where(row == place, 1.0, 0.0), here))
            panel_h, panel_l = split(jnp.concatenate(panel, axis=0))
            whole = jnp.dot(jnp.concatenate([wide_h, wide_h, wide_l], axis=1),
                            jnp.concatenate([panel_h, panel_l, panel_h], axis=0),
                            preferred_element_type=jnp.float32)
            for q in range(per):
                at = g * per + q
                part = whole[q * BASE:(q + 1) * BASE]
                fac_ref[at // by, at % by, low:high, :] = jnp.where(seg <= stage, part, 0.0).astype(fac_ref.dtype)
                if high < order:
                    h, l = split(part)
                    left = jnp.concatenate([h, h, l], axis=0).T
                    update = jnp.dot(left[high:], jnp.concatenate([h, l, h], axis=0), preferred_element_type=jnp.float32)
                    below = gs[at, high:, :]
                    below = jnp.where(lanes[high:] // BASE == stage, 0.0, below)
                    gs[at, high:, :] = below - update


def sum_kernel(fac_ref, v_ref, wt, out_ref, img, loc, px, py, pc, rx, ry, rc, send_sem, recv_sem):
    bx, by = fac_ref.shape[:2]
    there, exists = neighbours()
    sends = [px.at[0], px.at[1], py.at[0], py.at[1]] + [pc.at[k] for k in range(4)]
    lands = [rx.at[0], rx.at[1], ry.at[0], ry.at[1]] + [rc.at[k] for k in range(4)]
    barrier = pltpu.get_barrier_semaphore()
    for d in DIRS:
        @pl.when(exists(d))
        def _(d=d):
            pl.semaphore_signal(barrier, inc=1, device_id=there(d), device_id_type=MESH)
    for k, d in enumerate(DIRS):
        @pl.when(jnp.logical_not(exists((-d[0], -d[1]))))
        def _(k=k):
            lands[k][...] = jnp.zeros(lands[k].shape, lands[k].dtype)

    @pl.loop(0, by)
    def _(y):
        for x in range(bx):
            img[x, y] = lax.dot_general(fac_ref[x, y], v_ref[x, y], (((0,), (0,)), ((), ())),
                                        preferred_element_type=jnp.float32)

    def target(tx, ty):
        total = None
        for x in range(bx):
            for y in range(by):
                ax, ay = tx - x, ty - y
                if 0 <= ax < 3 and 0 <= ay < 3:
                    term = wt[ax * 3 + ay, x, pl.ds(y, 1), :] * img[x, y]
                    total = term if total is None else total + term
        return total

    for y in range(by):
        px[0, y] = target(bx + 1, y + 1).astype(px.dtype)
        px[1, y] = target(0, y + 1).astype(px.dtype)
    for k, d in enumerate(DIRS[4:]):
        pc[k] = target(bx + 1 if d[0] > 0 else 0, by + 1 if d[1] > 0 else 0).astype(pc.dtype)
    for x in range(bx):
        py[0, x] = target(x + 1, by + 1).astype(py.dtype)
        py[1, x] = target(x + 1, 0).astype(py.dtype)
    near = [exists(d).astype(jnp.int32) for d in DIRS[:4]]
    pl.semaphore_wait(barrier, (near[0] + near[1] + 1) * (near[2] + near[3] + 1) - 1)

    def copy(k, d):
        return pltpu.make_async_remote_copy(
            src_ref=sends[k], dst_ref=lands[k], send_sem=send_sem.at[k], recv_sem=recv_sem.at[k],
            device_id=there(d), device_id_type=MESH)

    order_of = (4, 5, 6, 7, 0, 1, 2, 3)
    for k in order_of:
        @pl.when(exists(DIRS[k]))
        def _(k=k):
            copy(k, DIRS[k]).start()
    for x in range(bx):
        for y in range(by):
            loc[x, y] = target(x + 1, y + 1)
    for k in order_of:
        @pl.when(exists((-DIRS[k][0], -DIRS[k][1])))
        def _(k=k):
            copy(k, DIRS[k]).wait_recv()
    for x in range(bx):
        for y in range(by):
            total = loc[x, y]
            for k, edge in ((0, 0), (1, bx - 1)):
                if x == edge:
                    total = total + rx[k, y].astype(jnp.float32)
            for k, edge in ((0, 0), (1, by - 1)):
                if y == edge:
                    total = total + ry[k, x].astype(jnp.float32)
            for k, place in enumerate(((0, 0), (0, by - 1), (bx - 1, 0), (bx - 1, by - 1))):
                if (x, y) == place:
                    total = total + rc[k].astype(jnp.float32)
            out_ref[x, y] = total.astype(out_ref.dtype)
    for k in order_of:
        @pl.when(exists(DIRS[k]))
        def _(k=k):
            copy(k, DIRS[k]).wait_send()


def local(coeffs, permit, shift_diag, codes, counts, weights, vectors):
    bx, by, coupling, order = coeffs.shape
    nv = vectors.shape[3]
    bf16, f32 = jnp.bfloat16, jnp.float32
    anyspace = pl.BlockSpec(memory_space=pl.ANY)
    vmem = pl.BlockSpec(memory_space=pltpu.VMEM)
    codes, weights = jnp.transpose(codes, (2, 0, 1)), jnp.transpose(weights, (2, 0, 1))
    wide = by + 2
    packed = order // 2 + order // 8
    copies = 2 * bx + 2 + 2 * by
    gram, sums = pl.pallas_call(
        gram_kernel,
        out_shape=(pltpu.VMEM((bx, by, order, order), f32), pltpu.VMEM((9, bx, by, order), f32)),
        in_specs=[anyspace] * 6,
        out_specs=(vmem, vmem),
        scratch_shapes=[
            pltpu.VMEM((bx * wide, coupling, order), bf16),
            pltpu.VMEM((bx * wide, order, coupling), bf16),
            pltpu.VMEM(permit.shape, f32), pltpu.VMEM(shift_diag.shape, f32),
            pltpu.VMEM(codes.shape, jnp.int32), pltpu.VMEM(counts.shape, jnp.int32), pltpu.VMEM(weights.shape, f32),
            pltpu.VMEM((order, order), f32),
            pltpu.VMEM((bx, 9, by, coupling), f32), pltpu.VMEM((2, 3, by, coupling), f32),
            pltpu.VMEM((2, by, packed, order), f32), pltpu.VMEM((2, by, packed, order), f32),
            pltpu.SemaphoreType.DMA((bx,)), pltpu.SemaphoreType.DMA((5,)),
            pltpu.SemaphoreType.DMA((copies,)), pltpu.SemaphoreType.DMA((copies,)),
        ],
        compiler_params=pltpu.CompilerParams(collective_id=0, has_side_effects=True),
        name="gram",
    )(coeffs, permit, shift_diag, codes, counts, weights)
    fac, held = pl.pallas_call(
        factor_kernel,
        out_shape=(jax.ShapeDtypeStruct((bx, by, order, order), bf16), pltpu.VMEM((bx, by, order, order), bf16)),
        in_specs=[vmem],
        out_specs=(anyspace, vmem),
        scratch_shapes=[pltpu.VMEM((bx * by, order, order), f32), pltpu.SemaphoreType.DMA],
        name="factor",
    )(pltpu.with_memory_space_constraint(gram, pltpu.VMEM))
    edges = [
        pltpu.VMEM((2, by, order, nv), bf16),
        pltpu.VMEM((2, bx, order, nv), bf16),
        pltpu.VMEM((4, order, nv), bf16),
    ]
    applied = pl.pallas_call(
        sum_kernel,
        out_shape=pltpu.VMEM((bx, by, order, nv), bf16),
        in_specs=[vmem, vmem, vmem],
        out_specs=vmem,
        scratch_shapes=[
            pltpu.VMEM((bx, by, order, nv), f32),
            pltpu.VMEM((bx, by, order, nv), f32),
            *edges, *edges,
            pltpu.SemaphoreType.DMA((8,)), pltpu.SemaphoreType.DMA((8,)),
        ],
        compiler_params=pltpu.CompilerParams(collective_id=1, has_side_effects=True),
        name="sums",
    )(pltpu.with_memory_space_constraint(held, pltpu.VMEM), vectors, pltpu.with_memory_space_constraint(sums, pltpu.VMEM))
    return fac, applied


def solution(mesh):
    placed = (
        P("gx", "gy", None, None),
        P("gx", "gy", None),
        P("gx", "gy", None),
        P("gx", "gy", None),
        P("gx", "gy"),
        P("gx", "gy", None),
        P("gx", "gy", None, None),
    )
    return jax.shard_map(
        local,
        mesh=mesh,
        in_specs=placed,
        out_specs=(P("gx", "gy", None, None), P("gx", "gy", None, None)),
        check_vma=False,
    )
```

```python
import functools

import jax
import jax.numpy as jnp
from jax import lax
from jax.experimental import pallas as pl
from jax.experimental.pallas import tpu as pltpu
from jax.sharding import PartitionSpec as P

MESH = pl.DeviceIdType.MESH
BASE = 32
WIDTH = 4
DIRS = ((1, 0), (-1, 0), (0, 1), (0, -1), (1, 1), (1, -1), (-1, 1), (-1, -1))


def neighbours():
    sizes = (lax.axis_size("gx"), lax.axis_size("gy"))
    me = (lax.axis_index("gx"), lax.axis_index("gy"))

    def there(d):
        return (me[0] + d[0], me[1] + d[1])

    def exists(d):
        ok = None
        for size, at, step in zip(sizes, me, d):
            if step == 0:
                continue
            test = (at + 1 < size) if step > 0 else (at > 0)
            ok = test if ok is None else jnp.logical_and(ok, test)
        return ok

    return there, exists


def gram_kernel(c_ref, permit_ref, shift_ref, codes_ref, counts_ref, weights_ref, gram_ref, wrow_ref,
                cs, ts, pm, sh, cd, ct, wg, flat, tp, tq, ps, pr, own_sem, in_sem, send_sem, recv_sem):
    bx, by, coupling, order = c_ref.shape
    slots = codes_ref.shape[0]
    wide = by + 2
    quarter = order // 4
    packed = pr.shape[2]
    there, exists = neighbours()
    edge = {1: by - 1, -1: 0}
    land = {1: 0, -1: by + 1}
    gx_dirs, gy_dirs = DIRS[:2], DIRS[2:4]
    small = [pltpu.make_async_copy(source, target, in_sem.at[k]) for k, (source, target) in enumerate((
        (codes_ref, cd), (counts_ref, ct), (weights_ref, wg), (permit_ref, pm), (shift_ref, sh)))]
    own = [pltpu.make_async_copy(c_ref.at[x], cs.at[pl.ds(x * wide + 1, by)], own_sem.at[x]) for x in range(bx)]
    barrier = pltpu.get_barrier_semaphore()
    for d in DIRS[:4]:
        @pl.when(exists(d))
        def _(d=d):
            pl.semaphore_signal(barrier, inc=1, device_id=there(d), device_id_type=MESH)
    for copy in small + own:
        copy.start()

    def remote(source, target, k, d):
        return pltpu.make_async_remote_copy(
            src_ref=source, dst_ref=target, send_sem=send_sem.at[k], recv_sem=recv_sem.at[k],
            device_id=there(d), device_id_type=MESH)

    def gy_copy(j, x):
        d = gy_dirs[j]
        return remote(c_ref.at[x, edge[d[1]]], cs.at[x * wide + land[d[1]]], j * bx + x, d)

    def scale_copy(j):
        x, o = ((bx - 1, 6), (0, 0))[j]
        return remote(tp.at[x, pl.ds(o, 3)], tq.at[j], 2 * bx + j, gx_dirs[j])

    def part_copy(j, y):
        return remote(ps.at[j, y], pr.at[j, y], 2 * bx + 2 + j * by + y, gx_dirs[1 - j])

    for copy in small[:4]:
        copy.wait()
    flat[...] = jnp.zeros(flat.shape, flat.dtype)
    half = order // 2
    for o in range(9):
        times = jnp.zeros((bx, by), jnp.float32)
        total = jnp.zeros((bx, by), jnp.float32)
        for s in range(slots):
            hit = (cd[s] == o) & (s < ct[...])
            times = times + jnp.where(hit, 1.0, 0.0)
            total = total + jnp.where(hit, wg[s], 0.0)
        flat[o * bx:(o + 1) * bx, 0:by] = times
        flat[half + o * bx:half + (o + 1) * bx, 0:by] = total
    turned = flat[...].T[0:by]

    def column(c):
        return jnp.take_along_axis(turned, jnp.full((by, order), c, jnp.int32), axis=1)

    for o in (6, 7, 8, 0, 1, 2, 3, 4, 5):
        for x in range(bx):
            times = column(o * bx + x)
            tp[x, o] = pm[x] * jnp.concatenate([times] * (coupling // order), axis=1)
            wrow_ref[o, x] = column(half + o * bx + x)

    near = [exists(d).astype(jnp.int32) for d in DIRS[:4]]
    pl.semaphore_wait(barrier, near[0] + near[1] + near[2] + near[3])
    for j, d in enumerate(gx_dirs):
        @pl.when(exists(d))
        def _(j=j):
            scale_copy(j).start()
    for j, d in enumerate(gy_dirs):
        @pl.when(exists(d))
        def _(j=j):
            for x in range(bx):
                gy_copy(j, x).start()

    zero = jnp.zeros((coupling, order), cs.dtype)
    for j, d in enumerate(gy_dirs):
        @pl.when(jnp.logical_not(exists((-d[0], -d[1]))))
        def _(d=d):
            for x in range(bx):
                cs[x * wide + land[d[1]]] = zero

    def turn(n):
        ts[n] = cs[n].T

    def terms(r, y, scales):
        left = jnp.concatenate([(ts[r * wide + y + ay].astype(jnp.float32) * scales(ay)).astype(jnp.bfloat16)
                                for ay in range(3)], axis=1)
        right = cs[pl.ds(r * wide + y, 3)].reshape(3 * coupling, order)
        return jnp.dot(left, right, preferred_element_type=jnp.float32)

    same = lax.broadcasted_iota(jnp.int32, (order, order), 0) == lax.broadcasted_iota(jnp.int32, (order, order), 1)

    def inner(y):
        for x in range(bx):
            acc = jnp.where(same, sh[x, pl.ds(y, 1), :], 0.0)
            for r in range(max(0, x - 1), min(bx, x + 2)):
                acc = acc + terms(r, y, lambda ay: tp[x, (r - x + 1) * 3 + ay, pl.ds(y, 1), :])
            gram_ref[x, y] = acc

    lane = lax.broadcasted_iota(jnp.int32, (quarter, order), 1)

    def outer(j, y):
        acc = terms((0, bx - 1)[j], y, lambda ay: tq[j, ay, pl.ds(y, 1), :])
        ps[j, y, 0:quarter] = acc[0:quarter]
        ps[j, y, quarter:2 * quarter] = jnp.where(
            lane < quarter, pltpu.roll(acc[3 * quarter:], quarter, axis=1), acc[quarter:2 * quarter])
        mid = 2 * quarter + quarter // 2
        ps[j, y, 2 * quarter:mid] = jnp.where(
            lane[:quarter // 2] < 2 * quarter, pltpu.roll(acc[mid:3 * quarter], 2 * quarter, axis=1), acc[2 * quarter:mid])

    def send(j, y):
        @pl.when(exists(gx_dirs[1 - j]))
        def _():
            part_copy(j, y).start()

    for copy in own:
        copy.wait()
    small[4].wait()
    for x in range(bx):
        @pl.loop(0, by, unroll=2)
        def _(y):
            turn(x * wide + y + 1)
    split_at = by // 2

    @pl.loop(1, split_at)
    def _(y):
        inner(y)

    for j in range(2):
        @pl.when(exists(gx_dirs[1 - j]))
        def _(j=j):
            scale_copy(j).wait_recv()
    for y in range(1, by - 1):
        for j in range(2):
            outer(j, y)
        for j in range(2):
            send(j, y)
    for j, d in enumerate(gy_dirs):
        @pl.when(exists((-d[0], -d[1])))
        def _(j=j):
            for x in range(bx):
                gy_copy(j, x).wait_recv()
    for x in range(bx):
        turn(x * wide)
        turn(x * wide + by + 1)
    for y in sorted({0, by - 1}):
        for j in range(2):
            outer(j, y)
        for j in range(2):
            send(j, y)

    @pl.loop(split_at, by - 1)
    def _(y):
        inner(y)

    @pl.loop(0, 2)
    def _(e):
        inner(e * (by - 1))

    mid = 2 * quarter + quarter // 2
    for y in list(range(1, by - 1)) + sorted({0, by - 1}):
        for j in range(2):
            @pl.when(exists(gx_dirs[j]))
            def _(j=j, y=y):
                part_copy(j, y).wait_recv()
                x = (bx - 1, 0)[j]
                gram_ref[x, y, 0:quarter] += pr[j, y, 0:quarter]
                both = pr[j, y, quarter:2 * quarter]
                gram_ref[x, y, quarter:2 * quarter] += both
                gram_ref[x, y, 3 * quarter:] += pltpu.roll(both, 3 * quarter, axis=1)
                both = pr[j, y, 2 * quarter:mid]
                gram_ref[x, y, 2 * quarter:mid] += both
                gram_ref[x, y, mid:3 * quarter] += pltpu.roll(both, 2 * quarter, axis=1)
    for j in range(2):
        @pl.when(exists(gx_dirs[j]))
        def _(j=j):
            scale_copy(j).wait_send()

        @pl.when(exists(gx_dirs[1 - j]))
        def _(j=j):
            for y in range(by):
                part_copy(j, y).wait_send()

        @pl.when(exists(gy_dirs[j]))
        def _(j=j):
            for x in range(bx):
                gy_copy(j, x).wait_send()


def split(x):
    h = x.astype(jnp.bfloat16)
    return h, (x - h.astype(jnp.float32)).astype(jnp.bfloat16)


def factor_kernel(gram_ref, v_ref, out_ref, fac_ref, held_ref, gs, v_sem, sem):
    bx, by, order = gram_ref.shape[:3]
    blocks = bx * by
    fetch = pltpu.make_async_copy(v_ref, held_ref, v_sem)
    fetch.start()
    for i in range(blocks):
        gs[i] = gram_ref[i // by, i % by]

    def put(stage):
        rows = pl.ds(stage * BASE, BASE)
        return pltpu.make_async_copy(fac_ref.at[:, :, rows], out_ref.at[:, :, rows], sem.at[stage])

    factor(gs, fac_ref, bx, by, order, put)
    for stage in range(order // BASE):
        put(stage).wait()
    fetch.wait()


def factor(gs, fac_ref, bx, by, order, put):
    blocks = bx * by
    lanes = lax.broadcasted_iota(jnp.int32, (order, order), 1)
    per = order // BASE
    seg = lax.broadcasted_iota(jnp.int32, (BASE, order), 1) // BASE
    place = lax.broadcasted_iota(jnp.int32, (BASE, order), 1) % BASE
    row = lax.broadcasted_iota(jnp.int32, (BASE, order), 0)
    seg8, place8, row8 = seg[:8], place[:8], row[:8]
    masks = [jnp.where(seg == q, 1.0, 0.0).astype(jnp.bfloat16) for q in range(per)]
    tops = BASE // 8
    groups = blocks // per
    for stage in range(per):
        low = stage * BASE
        high = low + BASE
        packs = []
        for g in range(groups):
            pack = None
            for q in range(per):
                piece = gs[g * per + q, low:high, :]
                shift = (q * BASE - low) % order
                piece = pltpu.roll(piece, shift, axis=1) if shift else piece
                pack = piece if pack is None else jnp.where(seg == q, piece, pack)
            packs.append([pack[8 * c:8 * c + 8] for c in range(tops)])
        pivots = [[jnp.ones((8, order), jnp.float32) for _ in range(tops)] for _ in range(groups)]
        for first in range(0, BASE, WIDTH):
            top = first // 8
            cols = [[[jnp.take_along_axis(m[c], seg8 * BASE + (first + j), axis=1) for c in range(top, tops)]
                     for j in range(WIDTH)] for m in packs]
            for j in range(WIDTH):
                k = first + j
                at = k - 8 * top
                for g, m in enumerate(packs):
                    f = cols[g][j]
                    d = jnp.broadcast_to(f[0][at:at + 1], (8, order))
                    inv_d = 1.0 / d
                    pivots[g][top] = jnp.where(row8 == at, d, pivots[g][top])
                    f = [jnp.where(row8 > at, f[0], 0.0)] + f[1:]
                    for n in range(j + 1, WIDTH):
                        t = jnp.broadcast_to(cols[g][n][0][at:at + 1], (8, order)) * inv_d
                        cols[g][n] = [x - y * t for x, y in zip(cols[g][n], f)]
                    r = (jnp.broadcast_to(m[top][at:at + 1], (8, order)) + jnp.where(place8 == k, 1.0, 0.0)) * inv_d
                    for c in range(top, tops):
                        m[c] = m[c] - f[c - top] * r
        for g, m in enumerate(packs):
            m = jnp.concatenate(m, axis=0)
            unit = jnp.where(row > place, m, jnp.where(row == place, 1.0, 0.0))
            inv = unit * lax.rsqrt(jnp.concatenate(pivots[g], axis=0))
            inv_h, inv_l = split(inv)
            wide_h = jnp.concatenate([inv_h * mask for mask in masks], axis=0)
            wide_l = jnp.concatenate([inv_l * mask for mask in masks], axis=0)
            panel = []
            for q in range(per):
                here = gs[g * per + q, low:high, :]
                panel.append(jnp.where(seg == stage, jnp.where(row == place, 1.0, 0.0), here))
            panel_h, panel_l = split(jnp.concatenate(panel, axis=0))
            whole = jnp.dot(jnp.concatenate([wide_h, wide_h, wide_l], axis=1),
                            jnp.concatenate([panel_h, panel_l, panel_h], axis=0),
                            preferred_element_type=jnp.float32)
            for q in range(per):
                at = g * per + q
                part = whole[q * BASE:(q + 1) * BASE]
                fac_ref[at // by, at % by, low:high, :] = jnp.where(seg <= stage, part, 0.0).astype(fac_ref.dtype)
                if high < order:
                    h, l = split(part)
                    left = jnp.concatenate([h, h, l], axis=0).T
                    update = jnp.dot(left[high:], jnp.concatenate([h, l, h], axis=0), preferred_element_type=jnp.float32)
                    below = gs[at, high:, :]
                    below = jnp.where(lanes[high:] // BASE == stage, 0.0, below)
                    gs[at, high:, :] = below - update
        put(stage).start()


def sum_kernel(fac_ref, v_ref, wt, out_ref, img, loc, px, py, rx, ry, send_sem, recv_sem):
    bx, by = fac_ref.shape[:2]
    there, exists = neighbours()
    gx_dirs, gy_dirs = DIRS[:2], DIRS[2:4]
    barrier = pltpu.get_barrier_semaphore()
    for d in DIRS[:4]:
        @pl.when(exists(d))
        def _(d=d):
            pl.semaphore_signal(barrier, inc=1, device_id=there(d), device_id_type=MESH)

    def remote(source, target, k, d):
        return pltpu.make_async_remote_copy(
            src_ref=source, dst_ref=target, send_sem=send_sem.at[k], recv_sem=recv_sem.at[k],
            device_id=there(d), device_id_type=MESH)

    def gx_copy(k, y):
        return remote(px.at[k, y], rx.at[k, y], k * by + y, gx_dirs[k])

    def gy_copy(k, x):
        return remote(py.at[k, x], ry.at[k, x], 2 * by + k * (bx + 2) + x, gy_dirs[k])

    def image(x, y):
        img[x, y] = lax.dot_general(fac_ref[x, y], v_ref[x, y], (((0,), (0,)), ((), ())),
                                    preferred_element_type=jnp.float32)

    def target(tx, ty):
        total = None
        for x in range(bx):
            for y in range(by):
                ax, ay = tx - x, ty - y
                if 0 <= ax < 3 and 0 <= ay < 3:
                    term = wt[ax * 3 + ay, x, pl.ds(y, 1), :] * img[x, y]
                    total = term if total is None else total + term
        return total

    rows = (bx + 1, 0)
    edges = (by - 1, 0)
    ends = sorted({0, by - 1})
    for y in ends:
        for x in range(bx):
            image(x, y)
    for k in range(2):
        for r in rows:
            py[k, r] = target(r, (by + 1, 0)[k]).astype(py.dtype)
    near = [exists(d).astype(jnp.int32) for d in DIRS[:4]]
    pl.semaphore_wait(barrier, near[0] + near[1] + near[2] + near[3])
    for k, d in enumerate(gy_dirs):
        @pl.when(exists(d))
        def _(k=k):
            for r in rows:
                gy_copy(k, r).start()

        @pl.when(jnp.logical_not(exists((-d[0], -d[1]))))
        def _(k=k):
            ry[k] = jnp.zeros(ry.shape[1:], ry.dtype)
    for k, d in enumerate(gx_dirs):
        @pl.when(jnp.logical_not(exists((-d[0], -d[1]))))
        def _(k=k):
            rx[k] = jnp.zeros(rx.shape[1:], rx.dtype)
    ready = set(ends)
    for y in range(1, by - 1):
        for n in (y - 1, y, y + 1):
            if n not in ready:
                ready.add(n)
                for x in range(bx):
                    image(x, n)
        for k, d in enumerate(gx_dirs):
            px[k, y] = target(rows[k], y + 1).astype(px.dtype)
        for k, d in enumerate(gx_dirs):
            @pl.when(exists(d))
            def _(k=k, y=y):
                gx_copy(k, y).start()
    for k in range(2):
        for x in range(1, bx + 1):
            py[k, x] = target(x, (by + 1, 0)[k]).astype(py.dtype)
    for k, d in enumerate(gy_dirs):
        @pl.when(exists(d))
        def _(k=k):
            for x in range(1, bx + 1):
                gy_copy(k, x).start()
    for y in ends:
        for x in range(bx):
            loc[x, y] = target(x + 1, y + 1)
    for k, d in enumerate(gy_dirs):
        @pl.when(exists((-d[0], -d[1])))
        def _(k=k):
            for r in rows:
                gy_copy(k, r).wait_recv()
    for y in ends:
        for k in range(2):
            total = target(rows[k], y + 1)
            for j in range(2):
                if y == edges[1 - j]:
                    total = total + ry[j, rows[k]].astype(jnp.float32)
            px[k, y] = total.astype(px.dtype)
        for k, d in enumerate(gx_dirs):
            @pl.when(exists(d))
            def _(k=k, y=y):
                gx_copy(k, y).start()
    for x in range(bx):
        for y in range(1, by - 1):
            loc[x, y] = target(x + 1, y + 1)
    for k, d in enumerate(gy_dirs):
        @pl.when(exists((-d[0], -d[1])))
        def _(k=k):
            for x in range(1, bx + 1):
                gy_copy(k, x).wait_recv()
    for y in list(range(1, by - 1)) + ends:
        for k, d in enumerate(gx_dirs):
            @pl.when(exists((-d[0], -d[1])))
            def _(k=k, y=y):
                gx_copy(k, y).wait_recv()
        for x in range(bx):
            total = loc[x, y]
            for k in range(2):
                if x == (0, bx - 1)[k]:
                    total = total + rx[k, y].astype(jnp.float32)
                if y == edges[1 - k]:
                    total = total + ry[k, x + 1].astype(jnp.float32)
            out_ref[x, y] = total.astype(out_ref.dtype)
    for k, d in enumerate(gx_dirs):
        @pl.when(exists(d))
        def _(k=k):
            for y in range(by):
                gx_copy(k, y).wait_send()
    for k, d in enumerate(gy_dirs):
        @pl.when(exists(d))
        def _(k=k):
            for x in range(bx + 2):
                gy_copy(k, x).wait_send()


def local(coeffs, permit, shift_diag, codes, counts, weights, vectors):
    bx, by, coupling, order = coeffs.shape
    nv = vectors.shape[3]
    bf16, f32 = jnp.bfloat16, jnp.float32
    anyspace = pl.BlockSpec(memory_space=pl.ANY)
    vmem = pl.BlockSpec(memory_space=pltpu.VMEM)
    codes, weights = jnp.transpose(codes, (2, 0, 1)), jnp.transpose(weights, (2, 0, 1))
    wide = by + 2
    packed = order // 2 + order // 8
    copies = 2 * bx + 2 + 2 * by
    gram, sums = pl.pallas_call(
        gram_kernel,
        out_shape=(pltpu.VMEM((bx, by, order, order), f32), pltpu.VMEM((9, bx, by, order), f32)),
        in_specs=[anyspace] * 6,
        out_specs=(vmem, vmem),
        scratch_shapes=[
            pltpu.VMEM((bx * wide, coupling, order), bf16),
            pltpu.VMEM((bx * wide, order, coupling), bf16),
            pltpu.VMEM(permit.shape, f32), pltpu.VMEM(shift_diag.shape, f32),
            pltpu.VMEM(codes.shape, jnp.int32), pltpu.VMEM(counts.shape, jnp.int32), pltpu.VMEM(weights.shape, f32),
            pltpu.VMEM((order, order), f32),
            pltpu.VMEM((bx, 9, by, coupling), f32), pltpu.VMEM((2, 3, by, coupling), f32),
            pltpu.VMEM((2, by, packed, order), f32), pltpu.VMEM((2, by, packed, order), f32),
            pltpu.SemaphoreType.DMA((bx,)), pltpu.SemaphoreType.DMA((5,)),
            pltpu.SemaphoreType.DMA((copies,)), pltpu.SemaphoreType.DMA((copies,)),
        ],
        compiler_params=pltpu.CompilerParams(collective_id=0, has_side_effects=True),
        name="gram",
    )(coeffs, permit, shift_diag, codes, counts, weights)
    fac, held, vecs = pl.pallas_call(
        factor_kernel,
        out_shape=(
            jax.ShapeDtypeStruct((bx, by, order, order), bf16),
            pltpu.VMEM((bx, by, order, order), bf16),
            pltpu.VMEM((bx, by, order, nv), bf16),
        ),
        in_specs=[vmem, anyspace],
        out_specs=(anyspace, vmem, vmem),
        scratch_shapes=[
            pltpu.VMEM((bx * by, order, order), f32), pltpu.SemaphoreType.DMA,
            pltpu.SemaphoreType.DMA((order // BASE,)),
        ],
        name="factor",
    )(pltpu.with_memory_space_constraint(gram, pltpu.VMEM), vectors)
    edges = [pltpu.VMEM((2, by, order, nv), bf16), pltpu.VMEM((2, bx + 2, order, nv), bf16)]
    copies = 2 * by + 2 * (bx + 2)
    applied = pl.pallas_call(
        sum_kernel,
        out_shape=pltpu.VMEM((bx, by, order, nv), bf16),
        in_specs=[vmem, vmem, vmem],
        out_specs=vmem,
        scratch_shapes=[
            pltpu.VMEM((bx, by, order, nv), f32),
            pltpu.VMEM((bx, by, order, nv), f32),
            *edges, *edges,
            pltpu.SemaphoreType.DMA((copies,)), pltpu.SemaphoreType.DMA((copies,)),
        ],
        compiler_params=pltpu.CompilerParams(collective_id=1, has_side_effects=True),
        name="sums",
    )(*(pltpu.with_memory_space_constraint(x, pltpu.VMEM) for x in (held, vecs, sums)))
    return fac, applied


def solution(mesh):
    placed = (
        P("gx", "gy", None, None),
        P("gx", "gy", None),
        P("gx", "gy", None),
        P("gx", "gy", None),
        P("gx", "gy"),
        P("gx", "gy", None),
        P("gx", "gy", None, None),
    )
    return jax.shard_map(
        local,
        mesh=mesh,
        in_specs=placed,
        out_specs=(P("gx", "gy", None, None), P("gx", "gy", None, None)),
        check_vma=False,
    )
```

```python
import functools

import jax
import jax.numpy as jnp
from jax import lax
from jax.experimental import pallas as pl
from jax.experimental.pallas import tpu as pltpu
from jax.sharding import PartitionSpec as P

MESH = pl.DeviceIdType.MESH
BASE = 32
WIDTH = 4
DIRS = ((1, 0), (-1, 0), (0, 1), (0, -1), (1, 1), (1, -1), (-1, 1), (-1, -1))


def neighbours():
    sizes = (lax.axis_size("gx"), lax.axis_size("gy"))
    me = (lax.axis_index("gx"), lax.axis_index("gy"))

    def there(d):
        return (me[0] + d[0], me[1] + d[1])

    def exists(d):
        ok = None
        for size, at, step in zip(sizes, me, d):
            if step == 0:
                continue
            test = (at + 1 < size) if step > 0 else (at > 0)
            ok = test if ok is None else jnp.logical_and(ok, test)
        return ok

    return there, exists


def gram_kernel(c_ref, permit_ref, shift_ref, codes_ref, counts_ref, weights_ref, gram_ref, wrow_ref,
                cs, ts, pm, sh, cd, ct, wg, flat, tp, tq, ps, pr, own_sem, in_sem, send_sem, recv_sem):
    bx, by, coupling, order = c_ref.shape
    slots = codes_ref.shape[0]
    wide = by + 2
    quarter = order // 4
    packed = pr.shape[2]
    there, exists = neighbours()
    edge = {1: by - 1, -1: 0}
    land = {1: 0, -1: by + 1}
    gx_dirs, gy_dirs = DIRS[:2], DIRS[2:4]
    small = [pltpu.make_async_copy(source, target, in_sem.at[k]) for k, (source, target) in enumerate((
        (codes_ref, cd), (counts_ref, ct), (weights_ref, wg), (permit_ref, pm), (shift_ref, sh)))]
    own = [pltpu.make_async_copy(c_ref.at[x], cs.at[pl.ds(x * wide + 1, by)], own_sem.at[x]) for x in range(bx)]
    barrier = pltpu.get_barrier_semaphore()
    for d in DIRS[:4]:
        @pl.when(exists(d))
        def _(d=d):
            pl.semaphore_signal(barrier, inc=1, device_id=there(d), device_id_type=MESH)
    for copy in small + own:
        copy.start()

    def remote(source, target, k, d):
        return pltpu.make_async_remote_copy(
            src_ref=source, dst_ref=target, send_sem=send_sem.at[k], recv_sem=recv_sem.at[k],
            device_id=there(d), device_id_type=MESH)

    def gy_copy(j, x):
        d = gy_dirs[j]
        return remote(c_ref.at[x, edge[d[1]]], cs.at[x * wide + land[d[1]]], j * bx + x, d)

    def scale_copy(j):
        x, o = ((bx - 1, 6), (0, 0))[j]
        return remote(tp.at[x, pl.ds(o, 3)], tq.at[j], 2 * bx + j, gx_dirs[j])

    def part_copy(j, y):
        return remote(ps.at[j, y], pr.at[j, y], 2 * bx + 2 + j * by + y, gx_dirs[1 - j])

    for copy in small[:4]:
        copy.wait()
    flat[...] = jnp.zeros(flat.shape, flat.dtype)
    half = order // 2
    for o in range(9):
        times = jnp.zeros((bx, by), jnp.float32)
        total = jnp.zeros((bx, by), jnp.float32)
        for s in range(slots):
            hit = (cd[s] == o) & (s < ct[...])
            times = times + jnp.where(hit, 1.0, 0.0)
            total = total + jnp.where(hit, wg[s], 0.0)
        flat[o * bx:(o + 1) * bx, 0:by] = times
        flat[half + o * bx:half + (o + 1) * bx, 0:by] = total
    turned = flat[...].T[0:by]

    def column(c):
        return jnp.take_along_axis(turned, jnp.full((by, order), c, jnp.int32), axis=1)

    for o in (6, 7, 8, 0, 1, 2, 3, 4, 5):
        for x in range(bx):
            times = column(o * bx + x)
            tp[x, o] = pm[x] * jnp.concatenate([times] * (coupling // order), axis=1)
            wrow_ref[o, x] = column(half + o * bx + x)

    near = [exists(d).astype(jnp.int32) for d in DIRS[:4]]
    pl.semaphore_wait(barrier, near[0] + near[1] + near[2] + near[3])
    for j, d in enumerate(gx_dirs):
        @pl.when(exists(d))
        def _(j=j):
            scale_copy(j).start()
    for j, d in enumerate(gy_dirs):
        @pl.when(exists(d))
        def _(j=j):
            for x in range(bx):
                gy_copy(j, x).start()

    zero = jnp.zeros((coupling, order), cs.dtype)
    for j, d in enumerate(gy_dirs):
        @pl.when(jnp.logical_not(exists((-d[0], -d[1]))))
        def _(d=d):
            for x in range(bx):
                cs[x * wide + land[d[1]]] = zero

    def turn(n):
        ts[n] = cs[n].T

    def scaled(n, scale):
        rows = jnp.broadcast_to(scale, (16, coupling)).astype(jnp.bfloat16)
        return (ts[n].reshape(order // 16, 16, coupling) * rows[None]).reshape(order, coupling)

    def terms(r, y, scales):
        left = jnp.concatenate([
            jnp.concatenate([scaled(r * wide + y + ay, scale(ay)) for ay in range(3)], axis=1) for scale in scales], axis=0)
        right = cs[pl.ds(r * wide + y, 3)].reshape(3 * coupling, order)
        return jnp.dot(left, right, preferred_element_type=jnp.float32)

    same = lax.broadcasted_iota(jnp.int32, (order, order), 0) == lax.broadcasted_iota(jnp.int32, (order, order), 1)

    def inner(y):
        accs = [jnp.where(same, sh[x, pl.ds(y, 1), :], 0.0) for x in range(bx)]
        for r in range(bx):
            targets = range(max(0, r - 1), min(bx, r + 2))
            out = terms(r, y, [lambda ay, x=x: tp[x, (r - x + 1) * 3 + ay, pl.ds(y, 1), :] for x in targets])
            for k, x in enumerate(targets):
                accs[x] = accs[x] + out[k * order:(k + 1) * order]
        for x in range(bx):
            gram_ref[x, y] = accs[x]

    lane = lax.broadcasted_iota(jnp.int32, (quarter, order), 1)

    def outer(j, y):
        acc = terms((0, bx - 1)[j], y, [lambda ay: tq[j, ay, pl.ds(y, 1), :]])
        ps[j, y, 0:quarter] = acc[0:quarter]
        ps[j, y, quarter:2 * quarter] = jnp.where(
            lane < quarter, pltpu.roll(acc[3 * quarter:], quarter, axis=1), acc[quarter:2 * quarter])
        mid = 2 * quarter + quarter // 2
        ps[j, y, 2 * quarter:mid] = jnp.where(
            lane[:quarter // 2] < 2 * quarter, pltpu.roll(acc[mid:3 * quarter], 2 * quarter, axis=1), acc[2 * quarter:mid])

    def send(ys):
        for j in range(2):
            @pl.when(exists(gx_dirs[1 - j]))
            def _(j=j):
                for y in ys:
                    part_copy(j, y).start()

    for copy in own:
        copy.wait()
    small[4].wait()
    for x in range(bx):
        @pl.loop(0, by, unroll=2)
        def _(y):
            turn(x * wide + y + 1)
    split_at = by // 2

    for y in range(1, split_at):
        inner(y)

    for j in range(2):
        @pl.when(exists(gx_dirs[1 - j]))
        def _(j=j):
            scale_copy(j).wait_recv()
    chunk = 3
    for low in range(1, by - 1, chunk):
        ys = range(low, min(low + chunk, by - 1))
        for y in ys:
            for j in range(2):
                outer(j, y)
        send(ys)
    for j, d in enumerate(gy_dirs):
        @pl.when(exists((-d[0], -d[1])))
        def _(j=j):
            for x in range(bx):
                gy_copy(j, x).wait_recv()
    for x in range(bx):
        turn(x * wide)
        turn(x * wide + by + 1)
    ends = sorted({0, by - 1})
    for y in ends:
        for j in range(2):
            outer(j, y)
    send(ends)
    for y in list(range(split_at, by - 1)) + ends:
        inner(y)

    mid = 2 * quarter + quarter // 2
    for y in list(range(1, by - 1)) + sorted({0, by - 1}):
        for j in range(2):
            @pl.when(exists(gx_dirs[j]))
            def _(j=j, y=y):
                part_copy(j, y).wait_recv()
                x = (bx - 1, 0)[j]
                gram_ref[x, y, 0:quarter] += pr[j, y, 0:quarter]
                both = pr[j, y, quarter:2 * quarter]
                gram_ref[x, y, quarter:2 * quarter] += both
                gram_ref[x, y, 3 * quarter:] += pltpu.roll(both, 3 * quarter, axis=1)
                both = pr[j, y, 2 * quarter:mid]
                gram_ref[x, y, 2 * quarter:mid] += both
                gram_ref[x, y, mid:3 * quarter] += pltpu.roll(both, 2 * quarter, axis=1)
    for j in range(2):
        @pl.when(exists(gx_dirs[j]))
        def _(j=j):
            scale_copy(j).wait_send()

        @pl.when(exists(gx_dirs[1 - j]))
        def _(j=j):
            for y in range(by):
                part_copy(j, y).wait_send()

        @pl.when(exists(gy_dirs[j]))
        def _(j=j):
            for x in range(bx):
                gy_copy(j, x).wait_send()


def split(x):
    h = x.astype(jnp.bfloat16)
    return h, (x - h.astype(jnp.float32)).astype(jnp.bfloat16)


def factor_kernel(gram_ref, v_ref, out_ref, fac_ref, held_ref, gs, v_sem, sem):
    bx, by, order = gram_ref.shape[:3]
    blocks = bx * by
    fetch = pltpu.make_async_copy(v_ref, held_ref, v_sem)
    fetch.start()
    for i in range(blocks):
        gs[i] = gram_ref[i // by, i % by]

    def put(stage):
        rows = pl.ds(stage * BASE, BASE)
        return pltpu.make_async_copy(fac_ref.at[:, :, rows], out_ref.at[:, :, rows], sem.at[stage])

    factor(gs, fac_ref, bx, by, order, put)
    for stage in range(order // BASE):
        put(stage).wait()
    fetch.wait()


def factor(gs, fac_ref, bx, by, order, put):
    blocks = bx * by
    lanes = lax.broadcasted_iota(jnp.int32, (order, order), 1)
    per = order // BASE
    seg = lax.broadcasted_iota(jnp.int32, (BASE, order), 1) // BASE
    place = lax.broadcasted_iota(jnp.int32, (BASE, order), 1) % BASE
    row = lax.broadcasted_iota(jnp.int32, (BASE, order), 0)
    seg8, place8, row8 = seg[:8], place[:8], row[:8]
    masks = [jnp.where(seg == q, 1.0, 0.0).astype(jnp.bfloat16) for q in range(per)]
    tops = BASE // 8
    groups = blocks // per
    for stage in range(per):
        low = stage * BASE
        high = low + BASE
        packs = []
        for g in range(groups):
            pack = None
            for q in range(per):
                piece = gs[g * per + q, low:high, :]
                shift = (q * BASE - low) % order
                piece = pltpu.roll(piece, shift, axis=1) if shift else piece
                pack = piece if pack is None else jnp.where(seg == q, piece, pack)
            packs.append([pack[8 * c:8 * c + 8] for c in range(tops)])
        pivots = [[jnp.ones((8, order), jnp.float32) for _ in range(tops)] for _ in range(groups)]
        for first in range(0, BASE, WIDTH):
            top = first // 8
            cols = [[[jnp.take_along_axis(m[c], seg8 * BASE + (first + j), axis=1) for c in range(top, tops)]
                     for j in range(WIDTH)] for m in packs]
            for j in range(WIDTH):
                k = first + j
                at = k - 8 * top
                for g, m in enumerate(packs):
                    f = cols[g][j]
                    d = jnp.broadcast_to(f[0][at:at + 1], (8, order))
                    inv_d = 1.0 / d
                    pivots[g][top] = jnp.where(row8 == at, d, pivots[g][top])
                    f = [jnp.where(row8 > at, f[0], 0.0)] + f[1:]
                    for n in range(j + 1, WIDTH):
                        t = jnp.broadcast_to(cols[g][n][0][at:at + 1], (8, order)) * inv_d
                        cols[g][n] = [x - y * t for x, y in zip(cols[g][n], f)]
                    r = (jnp.broadcast_to(m[top][at:at + 1], (8, order)) + jnp.where(place8 == k, 1.0, 0.0)) * inv_d
                    for c in range(top, tops):
                        m[c] = m[c] - f[c - top] * r
        for g, m in enumerate(packs):
            m = jnp.concatenate(m, axis=0)
            unit = jnp.where(row > place, m, jnp.where(row == place, 1.0, 0.0))
            inv = unit * lax.rsqrt(jnp.concatenate(pivots[g], axis=0))
            inv_h, inv_l = split(inv)
            wide_h = jnp.concatenate([inv_h * mask for mask in masks], axis=0)
            wide_l = jnp.concatenate([inv_l * mask for mask in masks], axis=0)
            panel = []
            for q in range(per):
                here = gs[g * per + q, low:high, :]
                panel.append(jnp.where(seg == stage, jnp.where(row == place, 1.0, 0.0), here))
            panel_h, panel_l = split(jnp.concatenate(panel, axis=0))
            whole = jnp.dot(jnp.concatenate([wide_h, wide_h, wide_l], axis=1),
                            jnp.concatenate([panel_h, panel_l, panel_h], axis=0),
                            preferred_element_type=jnp.float32)
            for q in range(per):
                at = g * per + q
                part = whole[q * BASE:(q + 1) * BASE]
                fac_ref[at // by, at % by, low:high, :] = jnp.where(seg <= stage, part, 0.0).astype(fac_ref.dtype)
                if high < order:
                    h, l = split(part)
                    left = jnp.concatenate([h, h, l], axis=0).T
                    update = jnp.dot(left[high:], jnp.concatenate([h, l, h], axis=0), preferred_element_type=jnp.float32)
                    below = gs[at, high:, :]
                    below = jnp.where(lanes[high:] // BASE == stage, 0.0, below)
                    gs[at, high:, :] = below - update
        put(stage).start()


def sum_kernel(fac_ref, v_ref, wt, out_ref, img, loc, px, py, rx, ry, send_sem, recv_sem):
    bx, by = fac_ref.shape[:2]
    there, exists = neighbours()
    gx_dirs, gy_dirs = DIRS[:2], DIRS[2:4]
    barrier = pltpu.get_barrier_semaphore()
    for d in DIRS[:4]:
        @pl.when(exists(d))
        def _(d=d):
            pl.semaphore_signal(barrier, inc=1, device_id=there(d), device_id_type=MESH)

    def remote(source, target, k, d):
        return pltpu.make_async_remote_copy(
            src_ref=source, dst_ref=target, send_sem=send_sem.at[k], recv_sem=recv_sem.at[k],
            device_id=there(d), device_id_type=MESH)

    def gx_copy(k, y):
        return remote(px.at[k, y], rx.at[k, y], k * by + y, gx_dirs[k])

    def gy_copy(k, x):
        return remote(py.at[k, x], ry.at[k, x], 2 * by + k * (bx + 2) + x, gy_dirs[k])

    def image(x, y):
        img[x, y] = lax.dot_general(fac_ref[x, y], v_ref[x, y], (((0,), (0,)), ((), ())),
                                    preferred_element_type=jnp.float32)

    def target(tx, ty):
        total = None
        for x in range(bx):
            for y in range(by):
                ax, ay = tx - x, ty - y
                if 0 <= ax < 3 and 0 <= ay < 3:
                    term = wt[ax * 3 + ay, x, pl.ds(y, 1), :] * img[x, y]
                    total = term if total is None else total + term
        return total

    rows = (bx + 1, 0)
    edges = (by - 1, 0)
    ends = sorted({0, by - 1})
    for y in ends:
        for x in range(bx):
            image(x, y)
    for k in range(2):
        for r in rows:
            py[k, r] = target(r, (by + 1, 0)[k]).astype(py.dtype)
    near = [exists(d).astype(jnp.int32) for d in DIRS[:4]]
    pl.semaphore_wait(barrier, near[0] + near[1] + near[2] + near[3])
    for k, d in enumerate(gy_dirs):
        @pl.when(exists(d))
        def _(k=k):
            for r in rows:
                gy_copy(k, r).start()

        @pl.when(jnp.logical_not(exists((-d[0], -d[1]))))
        def _(k=k):
            ry[k] = jnp.zeros(ry.shape[1:], ry.dtype)
    for k, d in enumerate(gx_dirs):
        @pl.when(jnp.logical_not(exists((-d[0], -d[1]))))
        def _(k=k):
            rx[k] = jnp.zeros(rx.shape[1:], rx.dtype)
    ready = set(ends)
    for y in range(1, by - 1):
        for n in (y - 1, y, y + 1):
            if n not in ready:
                ready.add(n)
                for x in range(bx):
                    image(x, n)
        for k, d in enumerate(gx_dirs):
            px[k, y] = target(rows[k], y + 1).astype(px.dtype)
        for k, d in enumerate(gx_dirs):
            @pl.when(exists(d))
            def _(k=k, y=y):
                gx_copy(k, y).start()
    for k in range(2):
        for x in range(1, bx + 1):
            py[k, x] = target(x, (by + 1, 0)[k]).astype(py.dtype)
    for k, d in enumerate(gy_dirs):
        @pl.when(exists(d))
        def _(k=k):
            for x in range(1, bx + 1):
                gy_copy(k, x).start()
    for y in ends:
        for x in range(bx):
            loc[x, y] = target(x + 1, y + 1)
    for k, d in enumerate(gy_dirs):
        @pl.when(exists((-d[0], -d[1])))
        def _(k=k):
            for r in rows:
                gy_copy(k, r).wait_recv()
    for y in ends:
        for k in range(2):
            total = target(rows[k], y + 1)
            for j in range(2):
                if y == edges[1 - j]:
                    total = total + ry[j, rows[k]].astype(jnp.float32)
            px[k, y] = total.astype(px.dtype)
        for k, d in enumerate(gx_dirs):
            @pl.when(exists(d))
            def _(k=k, y=y):
                gx_copy(k, y).start()
    for x in range(bx):
        for y in range(1, by - 1):
            loc[x, y] = target(x + 1, y + 1)
    for k, d in enumerate(gy_dirs):
        @pl.when(exists((-d[0], -d[1])))
        def _(k=k):
            for x in range(1, bx + 1):
                gy_copy(k, x).wait_recv()
    for y in list(range(1, by - 1)) + ends:
        for k, d in enumerate(gx_dirs):
            @pl.when(exists((-d[0], -d[1])))
            def _(k=k, y=y):
                gx_copy(k, y).wait_recv()
        for x in range(bx):
            total = loc[x, y]
            for k in range(2):
                if x == (0, bx - 1)[k]:
                    total = total + rx[k, y].astype(jnp.float32)
                if y == edges[1 - k]:
                    total = total + ry[k, x + 1].astype(jnp.float32)
            out_ref[x, y] = total.astype(out_ref.dtype)
    for k, d in enumerate(gx_dirs):
        @pl.when(exists(d))
        def _(k=k):
            for y in range(by):
                gx_copy(k, y).wait_send()
    for k, d in enumerate(gy_dirs):
        @pl.when(exists(d))
        def _(k=k):
            for x in range(bx + 2):
                gy_copy(k, x).wait_send()


def local(coeffs, permit, shift_diag, codes, counts, weights, vectors):
    bx, by, coupling, order = coeffs.shape
    nv = vectors.shape[3]
    bf16, f32 = jnp.bfloat16, jnp.float32
    anyspace = pl.BlockSpec(memory_space=pl.ANY)
    vmem = pl.BlockSpec(memory_space=pltpu.VMEM)
    codes, weights = jnp.transpose(codes, (2, 0, 1)), jnp.transpose(weights, (2, 0, 1))
    wide = by + 2
    packed = order // 2 + order // 8
    copies = 2 * bx + 2 + 2 * by
    gram, sums = pl.pallas_call(
        gram_kernel,
        out_shape=(pltpu.VMEM((bx, by, order, order), f32), pltpu.VMEM((9, bx, by, order), f32)),
        in_specs=[anyspace] * 6,
        out_specs=(vmem, vmem),
        scratch_shapes=[
            pltpu.VMEM((bx * wide, coupling, order), bf16),
            pltpu.VMEM((bx * wide, order, coupling), bf16),
            pltpu.VMEM(permit.shape, f32), pltpu.VMEM(shift_diag.shape, f32),
            pltpu.VMEM(codes.shape, jnp.int32), pltpu.VMEM(counts.shape, jnp.int32), pltpu.VMEM(weights.shape, f32),
            pltpu.VMEM((order, order), f32),
            pltpu.VMEM((bx, 9, by, coupling), f32), pltpu.VMEM((2, 3, by, coupling), f32),
            pltpu.VMEM((2, by, packed, order), f32), pltpu.VMEM((2, by, packed, order), f32),
            pltpu.SemaphoreType.DMA((bx,)), pltpu.SemaphoreType.DMA((5,)),
            pltpu.SemaphoreType.DMA((copies,)), pltpu.SemaphoreType.DMA((copies,)),
        ],
        compiler_params=pltpu.CompilerParams(collective_id=0, has_side_effects=True),
        name="gram",
    )(coeffs, permit, shift_diag, codes, counts, weights)
    fac, held, vecs = pl.pallas_call(
        factor_kernel,
        out_shape=(
            jax.ShapeDtypeStruct((bx, by, order, order), bf16),
            pltpu.VMEM((bx, by, order, order), bf16),
            pltpu.VMEM((bx, by, order, nv), bf16),
        ),
        in_specs=[vmem, anyspace],
        out_specs=(anyspace, vmem, vmem),
        scratch_shapes=[
            pltpu.VMEM((bx * by, order, order), f32), pltpu.SemaphoreType.DMA,
            pltpu.SemaphoreType.DMA((order // BASE,)),
        ],
        name="factor",
    )(pltpu.with_memory_space_constraint(gram, pltpu.VMEM), vectors)
    edges = [pltpu.VMEM((2, by, order, nv), bf16), pltpu.VMEM((2, bx + 2, order, nv), bf16)]
    copies = 2 * by + 2 * (bx + 2)
    applied = pl.pallas_call(
        sum_kernel,
        out_shape=pltpu.VMEM((bx, by, order, nv), bf16),
        in_specs=[vmem, vmem, vmem],
        out_specs=vmem,
        scratch_shapes=[
            pltpu.VMEM((bx, by, order, nv), f32),
            pltpu.VMEM((bx, by, order, nv), f32),
            *edges, *edges,
            pltpu.SemaphoreType.DMA((copies,)), pltpu.SemaphoreType.DMA((copies,)),
        ],
        compiler_params=pltpu.CompilerParams(collective_id=1, has_side_effects=True),
        name="sums",
    )(*(pltpu.with_memory_space_constraint(x, pltpu.VMEM) for x in (held, vecs, sums)))
    return fac, applied


def solution(mesh):
    placed = (
        P("gx", "gy", None, None),
        P("gx", "gy", None),
        P("gx", "gy", None),
        P("gx", "gy", None),
        P("gx", "gy"),
        P("gx", "gy", None),
        P("gx", "gy", None, None),
    )
    return jax.shard_map(
        local,
        mesh=mesh,
        in_specs=placed,
        out_specs=(P("gx", "gy", None, None), P("gx", "gy", None, None)),
        check_vma=False,
    )
```

```python
import functools

import jax
import jax.numpy as jnp
from jax import lax
from jax.experimental import pallas as pl
from jax.experimental.pallas import tpu as pltpu
from jax.sharding import PartitionSpec as P

MESH = pl.DeviceIdType.MESH
BASE = 32
WIDTH = 4
DIRS = ((1, 0), (-1, 0), (0, 1), (0, -1), (1, 1), (1, -1), (-1, 1), (-1, -1))


def neighbours():
    sizes = (lax.axis_size("gx"), lax.axis_size("gy"))
    me = (lax.axis_index("gx"), lax.axis_index("gy"))

    def there(d):
        return (me[0] + d[0], me[1] + d[1])

    def exists(d):
        ok = None
        for size, at, step in zip(sizes, me, d):
            if step == 0:
                continue
            test = (at + 1 < size) if step > 0 else (at > 0)
            ok = test if ok is None else jnp.logical_and(ok, test)
        return ok

    return there, exists


def gram_kernel(c_ref, permit_ref, shift_ref, codes_ref, counts_ref, weights_ref, gram_ref, wrow_ref,
                cs, ts, pm, sh, cd, ct, wg, flat, tp, tq, ps, pr, own_sem, in_sem, send_sem, recv_sem):
    bx, by, coupling, order = c_ref.shape
    slots = codes_ref.shape[0]
    wide = by + 2
    quarter = order // 4
    packed = pr.shape[2]
    there, exists = neighbours()
    edge = {1: by - 1, -1: 0}
    land = {1: 0, -1: by + 1}
    gx_dirs, gy_dirs = DIRS[:2], DIRS[2:4]
    small = [pltpu.make_async_copy(source, target, in_sem.at[k]) for k, (source, target) in enumerate((
        (codes_ref, cd), (counts_ref, ct), (weights_ref, wg), (permit_ref, pm), (shift_ref, sh)))]
    own = [pltpu.make_async_copy(c_ref.at[x], cs.at[pl.ds(x * wide + 1, by)], own_sem.at[x]) for x in range(bx)]
    barrier = pltpu.get_barrier_semaphore()
    for d in DIRS[:4]:
        @pl.when(exists(d))
        def _(d=d):
            pl.semaphore_signal(barrier, inc=1, device_id=there(d), device_id_type=MESH)
    for copy in small + own:
        copy.start()

    def remote(source, target, k, d):
        return pltpu.make_async_remote_copy(
            src_ref=source, dst_ref=target, send_sem=send_sem.at[k], recv_sem=recv_sem.at[k],
            device_id=there(d), device_id_type=MESH)

    def gy_copy(j, x):
        d = gy_dirs[j]
        return remote(c_ref.at[x, edge[d[1]]], cs.at[x * wide + land[d[1]]], j * bx + x, d)

    def scale_copy(j):
        x, o = ((bx - 1, 6), (0, 0))[j]
        return remote(tp.at[x, pl.ds(o, 3)], tq.at[j], 2 * bx + j, gx_dirs[j])

    def part_copy(j, y):
        return remote(ps.at[j, y], pr.at[j, y], 2 * bx + 2 + j * by + y, gx_dirs[1 - j])

    for copy in small[:4]:
        copy.wait()
    flat[...] = jnp.zeros(flat.shape, flat.dtype)
    half = order // 2
    for o in range(9):
        times = jnp.zeros((bx, by), jnp.float32)
        total = jnp.zeros((bx, by), jnp.float32)
        for s in range(slots):
            hit = (cd[s] == o) & (s < ct[...])
            times = times + jnp.where(hit, 1.0, 0.0)
            total = total + jnp.where(hit, wg[s], 0.0)
        flat[o * bx:(o + 1) * bx, 0:by] = times
        flat[half + o * bx:half + (o + 1) * bx, 0:by] = total
    turned = flat[...].T[0:by]

    def column(c):
        return jnp.take_along_axis(turned, jnp.full((by, order), c, jnp.int32), axis=1)

    def spread(x, o):
        times = column(o * bx + x)
        tp[x, o] = pm[x] * jnp.concatenate([times] * (coupling // order), axis=1)

    sent = [(bx - 1, o) for o in range(6, 9)] + [(0, o) for o in range(3)]
    for x, o in sent:
        spread(x, o)
    near = [exists(d).astype(jnp.int32) for d in DIRS[:4]]
    pl.semaphore_wait(barrier, near[0] + near[1] + near[2] + near[3])
    for j, d in enumerate(gx_dirs):
        @pl.when(exists(d))
        def _(j=j):
            scale_copy(j).start()
    for j, d in enumerate(gy_dirs):
        @pl.when(exists(d))
        def _(j=j):
            for x in range(bx):
                gy_copy(j, x).start()

    for o in range(9):
        for x in range(bx):
            if (x, o) not in sent:
                spread(x, o)
            wrow_ref[o, x] = column(half + o * bx + x)
    zero = jnp.zeros((coupling, order), cs.dtype)
    for j, d in enumerate(gy_dirs):
        @pl.when(jnp.logical_not(exists((-d[0], -d[1]))))
        def _(d=d):
            for x in range(bx):
                cs[x * wide + land[d[1]]] = zero

    def turn(n):
        ts[n] = cs[n].T

    def scaled(n, scale):
        rows = jnp.broadcast_to(scale, (16, coupling)).astype(jnp.bfloat16)
        return (ts[n].reshape(order // 16, 16, coupling) * rows[None]).reshape(order, coupling)

    def terms(r, y, scales):
        left = jnp.concatenate([
            jnp.concatenate([scaled(r * wide + y + ay, scale(ay)) for ay in range(3)], axis=1) for scale in scales], axis=0)
        right = cs[pl.ds(r * wide + y, 3)].reshape(3 * coupling, order)
        return jnp.dot(left, right, preferred_element_type=jnp.float32)

    same = lax.broadcasted_iota(jnp.int32, (order, order), 0) == lax.broadcasted_iota(jnp.int32, (order, order), 1)

    def inner(y):
        accs = [jnp.where(same, sh[x, pl.ds(y, 1), :], 0.0) for x in range(bx)]
        for r in range(bx):
            targets = range(max(0, r - 1), min(bx, r + 2))
            out = terms(r, y, [lambda ay, x=x: tp[x, (r - x + 1) * 3 + ay, pl.ds(y, 1), :] for x in targets])
            for k, x in enumerate(targets):
                accs[x] = accs[x] + out[k * order:(k + 1) * order]
        for x in range(bx):
            gram_ref[x, y] = accs[x]

    lane = lax.broadcasted_iota(jnp.int32, (quarter, order), 1)

    def outer(j, y):
        acc = terms((0, bx - 1)[j], y, [lambda ay: tq[j, ay, pl.ds(y, 1), :]])
        ps[j, y, 0:quarter] = acc[0:quarter]
        ps[j, y, quarter:2 * quarter] = jnp.where(
            lane < quarter, pltpu.roll(acc[3 * quarter:], quarter, axis=1), acc[quarter:2 * quarter])
        mid = 2 * quarter + quarter // 2
        ps[j, y, 2 * quarter:mid] = jnp.where(
            lane[:quarter // 2] < 2 * quarter, pltpu.roll(acc[mid:3 * quarter], 2 * quarter, axis=1), acc[2 * quarter:mid])

    def send(ys):
        for j in range(2):
            @pl.when(exists(gx_dirs[1 - j]))
            def _(j=j):
                for y in ys:
                    part_copy(j, y).start()

    for copy in own:
        copy.wait()
    small[4].wait()
    for x in range(bx):
        @pl.loop(0, by, unroll=2)
        def _(y):
            turn(x * wide + y + 1)

    for j in range(2):
        @pl.when(exists(gx_dirs[1 - j]))
        def _(j=j):
            scale_copy(j).wait_recv()
    chunk = 2
    for low in range(1, by - 1, chunk):
        ys = range(low, min(low + chunk, by - 1))
        for y in ys:
            for j in range(2):
                outer(j, y)
        send(ys)
    for j, d in enumerate(gy_dirs):
        @pl.when(exists((-d[0], -d[1])))
        def _(j=j):
            for x in range(bx):
                gy_copy(j, x).wait_recv()
    for x in range(bx):
        turn(x * wide)
        turn(x * wide + by + 1)
    ends = sorted({0, by - 1})
    for y in ends:
        for j in range(2):
            outer(j, y)
    send(ends)
    for y in list(range(1, by - 1)) + ends:
        inner(y)

    mid = 2 * quarter + quarter // 2
    for y in list(range(1, by - 1)) + sorted({0, by - 1}):
        for j in range(2):
            @pl.when(exists(gx_dirs[j]))
            def _(j=j, y=y):
                part_copy(j, y).wait_recv()
                x = (bx - 1, 0)[j]
                gram_ref[x, y, 0:quarter] += pr[j, y, 0:quarter]
                both = pr[j, y, quarter:2 * quarter]
                gram_ref[x, y, quarter:2 * quarter] += both
                gram_ref[x, y, 3 * quarter:] += pltpu.roll(both, 3 * quarter, axis=1)
                both = pr[j, y, 2 * quarter:mid]
                gram_ref[x, y, 2 * quarter:mid] += both
                gram_ref[x, y, mid:3 * quarter] += pltpu.roll(both, 2 * quarter, axis=1)
    for j in range(2):
        @pl.when(exists(gx_dirs[j]))
        def _(j=j):
            scale_copy(j).wait_send()

        @pl.when(exists(gx_dirs[1 - j]))
        def _(j=j):
            for y in range(by):
                part_copy(j, y).wait_send()

        @pl.when(exists(gy_dirs[j]))
        def _(j=j):
            for x in range(bx):
                gy_copy(j, x).wait_send()


def split(x):
    h = x.astype(jnp.bfloat16)
    return h, (x - h.astype(jnp.float32)).astype(jnp.bfloat16)


def factor_kernel(gram_ref, v_ref, out_ref, fac_ref, held_ref, gs, v_sem, sem):
    bx, by, order = gram_ref.shape[:3]
    blocks = bx * by
    fetch = pltpu.make_async_copy(v_ref, held_ref, v_sem)
    fetch.start()
    for i in range(blocks):
        gs[i] = gram_ref[i // by, i % by]

    def put(stage):
        rows = pl.ds(stage * BASE, BASE)
        return pltpu.make_async_copy(fac_ref.at[:, :, rows], out_ref.at[:, :, rows], sem.at[stage])

    factor(gs, fac_ref, bx, by, order, put)
    for stage in range(order // BASE):
        put(stage).wait()
    fetch.wait()


def factor(gs, fac_ref, bx, by, order, put):
    blocks = bx * by
    lanes = lax.broadcasted_iota(jnp.int32, (order, order), 1)
    per = order // BASE
    seg = lax.broadcasted_iota(jnp.int32, (BASE, order), 1) // BASE
    place = lax.broadcasted_iota(jnp.int32, (BASE, order), 1) % BASE
    row = lax.broadcasted_iota(jnp.int32, (BASE, order), 0)
    seg8, place8, row8 = seg[:8], place[:8], row[:8]
    masks = [jnp.where(seg == q, 1.0, 0.0).astype(jnp.bfloat16) for q in range(per)]
    tops = BASE // 8
    groups = blocks // per
    for stage in range(per):
        low = stage * BASE
        high = low + BASE
        packs = []
        for g in range(groups):
            pack = None
            for q in range(per):
                piece = gs[g * per + q, low:high, :]
                shift = (q * BASE - low) % order
                piece = pltpu.roll(piece, shift, axis=1) if shift else piece
                pack = piece if pack is None else jnp.where(seg == q, piece, pack)
            packs.append([pack[8 * c:8 * c + 8] for c in range(tops)])
        pivots = [[jnp.ones((8, order), jnp.float32) for _ in range(tops)] for _ in range(groups)]
        for first in range(0, BASE, WIDTH):
            top = first // 8
            cols = [[[jnp.take_along_axis(m[c], seg8 * BASE + (first + j), axis=1) for c in range(top, tops)]
                     for j in range(WIDTH)] for m in packs]
            for j in range(WIDTH):
                k = first + j
                at = k - 8 * top
                for g, m in enumerate(packs):
                    f = cols[g][j]
                    d = jnp.broadcast_to(f[0][at:at + 1], (8, order))
                    inv_d = 1.0 / d
                    pivots[g][top] = jnp.where(row8 == at, d, pivots[g][top])
                    f = [jnp.where(row8 > at, f[0], 0.0)] + f[1:]
                    for n in range(j + 1, WIDTH):
                        t = jnp.broadcast_to(cols[g][n][0][at:at + 1], (8, order)) * inv_d
                        cols[g][n] = [x - y * t for x, y in zip(cols[g][n], f)]
                    r = (jnp.broadcast_to(m[top][at:at + 1], (8, order)) + jnp.where(place8 == k, 1.0, 0.0)) * inv_d
                    for c in range(top, tops):
                        m[c] = m[c] - f[c - top] * r
        for g, m in enumerate(packs):
            m = jnp.concatenate(m, axis=0)
            unit = jnp.where(row > place, m, jnp.where(row == place, 1.0, 0.0))
            inv = unit * lax.rsqrt(jnp.concatenate(pivots[g], axis=0))
            inv_h, inv_l = split(inv)
            wide_h = jnp.concatenate([inv_h * mask for mask in masks], axis=0)
            wide_l = jnp.concatenate([inv_l * mask for mask in masks], axis=0)
            panel = []
            for q in range(per):
                here = gs[g * per + q, low:high, :]
                panel.append(jnp.where(seg == stage, jnp.where(row == place, 1.0, 0.0), here))
            panel_h, panel_l = split(jnp.concatenate(panel, axis=0))
            whole = jnp.dot(jnp.concatenate([wide_h, wide_h, wide_l], axis=1),
                            jnp.concatenate([panel_h, panel_l, panel_h], axis=0),
                            preferred_element_type=jnp.float32)
            for q in range(per):
                at = g * per + q
                part = whole[q * BASE:(q + 1) * BASE]
                fac_ref[at // by, at % by, low:high, :] = jnp.where(seg <= stage, part, 0.0).astype(fac_ref.dtype)
                if high < order:
                    h, l = split(part)
                    left = jnp.concatenate([h, h, l], axis=0).T
                    update = jnp.dot(left[high:], jnp.concatenate([h, l, h], axis=0), preferred_element_type=jnp.float32)
                    below = gs[at, high:, :]
                    below = jnp.where(lanes[high:] // BASE == stage, 0.0, below)
                    gs[at, high:, :] = below - update
        put(stage).start()


def sum_kernel(fac_ref, v_ref, wt, out_ref, img, loc, px, py, rx, ry, send_sem, recv_sem):
    bx, by = fac_ref.shape[:2]
    there, exists = neighbours()
    gx_dirs, gy_dirs = DIRS[:2], DIRS[2:4]
    barrier = pltpu.get_barrier_semaphore()
    for d in DIRS[:4]:
        @pl.when(exists(d))
        def _(d=d):
            pl.semaphore_signal(barrier, inc=1, device_id=there(d), device_id_type=MESH)

    def remote(source, target, k, d):
        return pltpu.make_async_remote_copy(
            src_ref=source, dst_ref=target, send_sem=send_sem.at[k], recv_sem=recv_sem.at[k],
            device_id=there(d), device_id_type=MESH)

    def gx_copy(k, y):
        return remote(px.at[k, y], rx.at[k, y], k * by + y, gx_dirs[k])

    def gy_copy(k, x):
        return remote(py.at[k, x], ry.at[k, x], 2 * by + k * (bx + 2) + x, gy_dirs[k])

    def image(x, y):
        img[x, y] = lax.dot_general(fac_ref[x, y], v_ref[x, y], (((0,), (0,)), ((), ())),
                                    preferred_element_type=jnp.float32)

    def target(tx, ty):
        total = None
        for x in range(bx):
            for y in range(by):
                ax, ay = tx - x, ty - y
                if 0 <= ax < 3 and 0 <= ay < 3:
                    term = wt[ax * 3 + ay, x, pl.ds(y, 1), :] * img[x, y]
                    total = term if total is None else total + term
        return total

    rows = (bx + 1, 0)
    edges = (by - 1, 0)
    ends = sorted({0, by - 1})
    for y in ends:
        for x in range(bx):
            image(x, y)
    for k in range(2):
        for r in rows:
            py[k, r] = target(r, (by + 1, 0)[k]).astype(py.dtype)
    near = [exists(d).astype(jnp.int32) for d in DIRS[:4]]
    pl.semaphore_wait(barrier, near[0] + near[1] + near[2] + near[3])
    for k, d in enumerate(gy_dirs):
        @pl.when(exists(d))
        def _(k=k):
            for r in rows:
                gy_copy(k, r).start()

        @pl.when(jnp.logical_not(exists((-d[0], -d[1]))))
        def _(k=k):
            ry[k] = jnp.zeros(ry.shape[1:], ry.dtype)
    for k, d in enumerate(gx_dirs):
        @pl.when(jnp.logical_not(exists((-d[0], -d[1]))))
        def _(k=k):
            rx[k] = jnp.zeros(rx.shape[1:], rx.dtype)
    ready = set(ends)
    for y in range(1, by - 1):
        for n in (y - 1, y, y + 1):
            if n not in ready:
                ready.add(n)
                for x in range(bx):
                    image(x, n)
        for k, d in enumerate(gx_dirs):
            px[k, y] = target(rows[k], y + 1).astype(px.dtype)
        for k, d in enumerate(gx_dirs):
            @pl.when(exists(d))
            def _(k=k, y=y):
                gx_copy(k, y).start()
    for k in range(2):
        for x in range(1, bx + 1):
            py[k, x] = target(x, (by + 1, 0)[k]).astype(py.dtype)
    for k, d in enumerate(gy_dirs):
        @pl.when(exists(d))
        def _(k=k):
            for x in range(1, bx + 1):
                gy_copy(k, x).start()
    for y in ends:
        for x in range(bx):
            loc[x, y] = target(x + 1, y + 1)
    for k, d in enumerate(gy_dirs):
        @pl.when(exists((-d[0], -d[1])))
        def _(k=k):
            for r in rows:
                gy_copy(k, r).wait_recv()
    for y in ends:
        for k in range(2):
            total = target(rows[k], y + 1)
            for j in range(2):
                if y == edges[1 - j]:
                    total = total + ry[j, rows[k]].astype(jnp.float32)
            px[k, y] = total.astype(px.dtype)
        for k, d in enumerate(gx_dirs):
            @pl.when(exists(d))
            def _(k=k, y=y):
                gx_copy(k, y).start()
    for x in range(bx):
        for y in range(1, by - 1):
            loc[x, y] = target(x + 1, y + 1)
    for k, d in enumerate(gy_dirs):
        @pl.when(exists((-d[0], -d[1])))
        def _(k=k):
            for x in range(1, bx + 1):
                gy_copy(k, x).wait_recv()
    for y in list(range(1, by - 1)) + ends:
        for k, d in enumerate(gx_dirs):
            @pl.when(exists((-d[0], -d[1])))
            def _(k=k, y=y):
                gx_copy(k, y).wait_recv()
        for x in range(bx):
            total = loc[x, y]
            for k in range(2):
                if x == (0, bx - 1)[k]:
                    total = total + rx[k, y].astype(jnp.float32)
                if y == edges[1 - k]:
                    total = total + ry[k, x + 1].astype(jnp.float32)
            out_ref[x, y] = total.astype(out_ref.dtype)
    for k, d in enumerate(gx_dirs):
        @pl.when(exists(d))
        def _(k=k):
            for y in range(by):
                gx_copy(k, y).wait_send()
    for k, d in enumerate(gy_dirs):
        @pl.when(exists(d))
        def _(k=k):
            for x in range(bx + 2):
                gy_copy(k, x).wait_send()


def local(coeffs, permit, shift_diag, codes, counts, weights, vectors):
    bx, by, coupling, order = coeffs.shape
    nv = vectors.shape[3]
    bf16, f32 = jnp.bfloat16, jnp.float32
    anyspace = pl.BlockSpec(memory_space=pl.ANY)
    vmem = pl.BlockSpec(memory_space=pltpu.VMEM)
    codes, weights = jnp.transpose(codes, (2, 0, 1)), jnp.transpose(weights, (2, 0, 1))
    wide = by + 2
    packed = order // 2 + order // 8
    copies = 2 * bx + 2 + 2 * by
    gram, sums = pl.pallas_call(
        gram_kernel,
        out_shape=(pltpu.VMEM((bx, by, order, order), f32), pltpu.VMEM((9, bx, by, order), f32)),
        in_specs=[anyspace] * 6,
        out_specs=(vmem, vmem),
        scratch_shapes=[
            pltpu.VMEM((bx * wide, coupling, order), bf16),
            pltpu.VMEM((bx * wide, order, coupling), bf16),
            pltpu.VMEM(permit.shape, f32), pltpu.VMEM(shift_diag.shape, f32),
            pltpu.VMEM(codes.shape, jnp.int32), pltpu.VMEM(counts.shape, jnp.int32), pltpu.VMEM(weights.shape, f32),
            pltpu.VMEM((order, order), f32),
            pltpu.VMEM((bx, 9, by, coupling), f32), pltpu.VMEM((2, 3, by, coupling), f32),
            pltpu.VMEM((2, by, packed, order), f32), pltpu.VMEM((2, by, packed, order), f32),
            pltpu.SemaphoreType.DMA((bx,)), pltpu.SemaphoreType.DMA((5,)),
            pltpu.SemaphoreType.DMA((copies,)), pltpu.SemaphoreType.DMA((copies,)),
        ],
        compiler_params=pltpu.CompilerParams(collective_id=0, has_side_effects=True),
        name="gram",
    )(coeffs, permit, shift_diag, codes, counts, weights)
    fac, held, vecs = pl.pallas_call(
        factor_kernel,
        out_shape=(
            jax.ShapeDtypeStruct((bx, by, order, order), bf16),
            pltpu.VMEM((bx, by, order, order), bf16),
            pltpu.VMEM((bx, by, order, nv), bf16),
        ),
        in_specs=[vmem, anyspace],
        out_specs=(anyspace, vmem, vmem),
        scratch_shapes=[
            pltpu.VMEM((bx * by, order, order), f32), pltpu.SemaphoreType.DMA,
            pltpu.SemaphoreType.DMA((order // BASE,)),
        ],
        name="factor",
    )(pltpu.with_memory_space_constraint(gram, pltpu.VMEM), vectors)
    edges = [pltpu.VMEM((2, by, order, nv), bf16), pltpu.VMEM((2, bx + 2, order, nv), bf16)]
    copies = 2 * by + 2 * (bx + 2)
    applied = pl.pallas_call(
        sum_kernel,
        out_shape=pltpu.VMEM((bx, by, order, nv), bf16),
        in_specs=[vmem, vmem, vmem],
        out_specs=vmem,
        scratch_shapes=[
            pltpu.VMEM((bx, by, order, nv), f32),
            pltpu.VMEM((bx, by, order, nv), f32),
            *edges, *edges,
            pltpu.SemaphoreType.DMA((copies,)), pltpu.SemaphoreType.DMA((copies,)),
        ],
        compiler_params=pltpu.CompilerParams(collective_id=1, has_side_effects=True),
        name="sums",
    )(*(pltpu.with_memory_space_constraint(x, pltpu.VMEM) for x in (held, vecs, sums)))
    return fac, applied


def solution(mesh):
    placed = (
        P("gx", "gy", None, None),
        P("gx", "gy", None),
        P("gx", "gy", None),
        P("gx", "gy", None),
        P("gx", "gy"),
        P("gx", "gy", None),
        P("gx", "gy", None, None),
    )
    return jax.shard_map(
        local,
        mesh=mesh,
        in_specs=placed,
        out_specs=(P("gx", "gy", None, None), P("gx", "gy", None, None)),
        check_vma=False,
    )
```

```python
import functools

import jax
import jax.numpy as jnp
from jax import lax
from jax.experimental import pallas as pl
from jax.experimental.pallas import tpu as pltpu
from jax.sharding import PartitionSpec as P

MESH = pl.DeviceIdType.MESH
BASE = 32
WIDTH = 4
DIRS = ((1, 0), (-1, 0), (0, 1), (0, -1), (1, 1), (1, -1), (-1, 1), (-1, -1))


def neighbours():
    sizes = (lax.axis_size("gx"), lax.axis_size("gy"))
    me = (lax.axis_index("gx"), lax.axis_index("gy"))

    def there(d):
        return (me[0] + d[0], me[1] + d[1])

    def exists(d):
        ok = None
        for size, at, step in zip(sizes, me, d):
            if step == 0:
                continue
            test = (at + 1 < size) if step > 0 else (at > 0)
            ok = test if ok is None else jnp.logical_and(ok, test)
        return ok

    return there, exists


def gram_kernel(c_ref, permit_ref, shift_ref, codes_ref, counts_ref, weights_ref, gram_ref, wrow_ref,
                cs, ts, pm, sh, cd, ct, wg, flat, tp, tb, tq, ps, pr, own_sem, in_sem, send_sem, recv_sem):
    bx, by, coupling, order = c_ref.shape
    slots = codes_ref.shape[0]
    wide = by + 2
    quarter = order // 4
    packed = pr.shape[2]
    there, exists = neighbours()
    edge = {1: by - 1, -1: 0}
    land = {1: 0, -1: by + 1}
    gx_dirs, gy_dirs = DIRS[:2], DIRS[2:4]
    small = [pltpu.make_async_copy(source, target, in_sem.at[k]) for k, (source, target) in enumerate((
        (codes_ref, cd), (counts_ref, ct), (weights_ref, wg), (permit_ref, pm), (shift_ref, sh)))]
    own = [pltpu.make_async_copy(c_ref.at[x], cs.at[pl.ds(x * wide + 1, by)], own_sem.at[x]) for x in range(bx)]
    barrier = pltpu.get_barrier_semaphore()
    for d in DIRS[:4]:
        @pl.when(exists(d))
        def _(d=d):
            pl.semaphore_signal(barrier, inc=1, device_id=there(d), device_id_type=MESH)
    for copy in small + own:
        copy.start()

    def remote(source, target, k, d):
        return pltpu.make_async_remote_copy(
            src_ref=source, dst_ref=target, send_sem=send_sem.at[k], recv_sem=recv_sem.at[k],
            device_id=there(d), device_id_type=MESH)

    def gy_copy(j, x):
        d = gy_dirs[j]
        return remote(c_ref.at[x, edge[d[1]]], cs.at[x * wide + land[d[1]]], j * bx + x, d)

    def scale_copy(j):
        return remote(tb.at[j], tq.at[j], 2 * bx + j, gx_dirs[j])

    def part_copy(j, y):
        return remote(ps.at[j, y], pr.at[j, y], 2 * bx + 2 + j * by + y, gx_dirs[1 - j])

    for copy in small[:4]:
        copy.wait()
    flat[...] = jnp.zeros(flat.shape, flat.dtype)
    half = order // 2
    for o in range(9):
        times = jnp.zeros((bx, by), jnp.float32)
        total = jnp.zeros((bx, by), jnp.float32)
        for s in range(slots):
            hit = (cd[s] == o) & (s < ct[...])
            times = times + jnp.where(hit, 1.0, 0.0)
            total = total + jnp.where(hit, wg[s], 0.0)
        flat[o * bx:(o + 1) * bx, 0:by] = times
        flat[half + o * bx:half + (o + 1) * bx, 0:by] = total
    turned = flat[...].T[0:by]

    def column(c):
        return jnp.take_along_axis(turned, jnp.full((by, order), c, jnp.int32), axis=1)

    def spread(x, o):
        times = column(o * bx + x)
        tp[x, o] = pm[x] * jnp.concatenate([times] * (coupling // order), axis=1)

    sent = [(bx - 1, o) for o in range(6, 9)] + [(0, o) for o in range(3)]
    for n, (x, o) in enumerate(sent):
        spread(x, o)
        tb[n // 3, n % 3] = tp[x, o].astype(tb.dtype)
    near = [exists(d).astype(jnp.int32) for d in DIRS[:4]]
    pl.semaphore_wait(barrier, near[0] + near[1] + near[2] + near[3])
    for j, d in enumerate(gx_dirs):
        @pl.when(exists(d))
        def _(j=j):
            scale_copy(j).start()
    for j, d in enumerate(gy_dirs):
        @pl.when(exists(d))
        def _(j=j):
            for x in range(bx):
                gy_copy(j, x).start()

    for o in range(9):
        for x in range(bx):
            if (x, o) not in sent:
                spread(x, o)
            wrow_ref[o, x] = column(half + o * bx + x)
    zero = jnp.zeros((coupling, order), cs.dtype)
    for j, d in enumerate(gy_dirs):
        @pl.when(jnp.logical_not(exists((-d[0], -d[1]))))
        def _(d=d):
            for x in range(bx):
                cs[x * wide + land[d[1]]] = zero

    def turn(n):
        ts[n] = cs[n].T

    def scaled(n, scale):
        rows = jnp.broadcast_to(scale, (16, coupling)).astype(jnp.bfloat16)
        return (ts[n].reshape(order // 16, 16, coupling) * rows[None]).reshape(order, coupling)

    def terms(r, y, scales):
        left = jnp.concatenate([
            jnp.concatenate([scaled(r * wide + y + ay, scale(ay)) for ay in range(3)], axis=1) for scale in scales], axis=0)
        right = cs[pl.ds(r * wide + y, 3)].reshape(3 * coupling, order)
        return jnp.dot(left, right, preferred_element_type=jnp.float32)

    same = lax.broadcasted_iota(jnp.int32, (order, order), 0) == lax.broadcasted_iota(jnp.int32, (order, order), 1)

    def inner(y):
        accs = [jnp.where(same, sh[x, pl.ds(y, 1), :], 0.0) for x in range(bx)]
        for r in range(bx):
            targets = range(max(0, r - 1), min(bx, r + 2))
            out = terms(r, y, [lambda ay, x=x: tp[x, (r - x + 1) * 3 + ay, pl.ds(y, 1), :] for x in targets])
            for k, x in enumerate(targets):
                accs[x] = accs[x] + out[k * order:(k + 1) * order]
        for x in range(bx):
            gram_ref[x, y] = accs[x]

    lane = lax.broadcasted_iota(jnp.int32, (quarter, order), 1)

    def outer(j, y):
        acc = terms((0, bx - 1)[j], y, [lambda ay: tq[j, ay].astype(jnp.float32)[y:y + 1]])
        ps[j, y, 0:quarter] = acc[0:quarter]
        ps[j, y, quarter:2 * quarter] = jnp.where(
            lane < quarter, pltpu.roll(acc[3 * quarter:], quarter, axis=1), acc[quarter:2 * quarter])
        mid = 2 * quarter + quarter // 2
        ps[j, y, 2 * quarter:mid] = jnp.where(
            lane[:quarter // 2] < 2 * quarter, pltpu.roll(acc[mid:3 * quarter], 2 * quarter, axis=1), acc[2 * quarter:mid])

    def send(ys):
        for j in range(2):
            @pl.when(exists(gx_dirs[1 - j]))
            def _(j=j):
                for y in ys:
                    part_copy(j, y).start()

    for copy in own:
        copy.wait()
    small[4].wait()
    for x in range(bx):
        @pl.loop(0, by, unroll=2)
        def _(y):
            turn(x * wide + y + 1)

    for j in range(2):
        @pl.when(exists(gx_dirs[1 - j]))
        def _(j=j):
            scale_copy(j).wait_recv()
    low = 1
    while low < by - 1:
        ys = range(low, min(2 * low, by - 1))
        low = ys[-1] + 1
        for y in ys:
            for j in range(2):
                outer(j, y)
        send(ys)
    for j, d in enumerate(gy_dirs):
        @pl.when(exists((-d[0], -d[1])))
        def _(j=j):
            for x in range(bx):
                gy_copy(j, x).wait_recv()
    for x in range(bx):
        turn(x * wide)
        turn(x * wide + by + 1)
    ends = sorted({0, by - 1})
    for y in ends:
        for j in range(2):
            outer(j, y)
    send(ends)
    for y in list(range(1, by - 1)) + ends:
        inner(y)

    mid = 2 * quarter + quarter // 2
    for y in list(range(1, by - 1)) + sorted({0, by - 1}):
        for j in range(2):
            @pl.when(exists(gx_dirs[j]))
            def _(j=j, y=y):
                part_copy(j, y).wait_recv()
                x = (bx - 1, 0)[j]
                gram_ref[x, y, 0:quarter] += pr[j, y, 0:quarter]
                both = pr[j, y, quarter:2 * quarter]
                gram_ref[x, y, quarter:2 * quarter] += both
                gram_ref[x, y, 3 * quarter:] += pltpu.roll(both, 3 * quarter, axis=1)
                both = pr[j, y, 2 * quarter:mid]
                gram_ref[x, y, 2 * quarter:mid] += both
                gram_ref[x, y, mid:3 * quarter] += pltpu.roll(both, 2 * quarter, axis=1)
    for j in range(2):
        @pl.when(exists(gx_dirs[j]))
        def _(j=j):
            scale_copy(j).wait_send()

        @pl.when(exists(gx_dirs[1 - j]))
        def _(j=j):
            for y in range(by):
                part_copy(j, y).wait_send()

        @pl.when(exists(gy_dirs[j]))
        def _(j=j):
            for x in range(bx):
                gy_copy(j, x).wait_send()


def split(x):
    h = x.astype(jnp.bfloat16)
    return h, (x - h.astype(jnp.float32)).astype(jnp.bfloat16)


def factor_kernel(gram_ref, v_ref, out_ref, fac_ref, held_ref, gs, v_sem, sem):
    bx, by, order = gram_ref.shape[:3]
    blocks = bx * by
    fetch = pltpu.make_async_copy(v_ref, held_ref, v_sem)
    fetch.start()
    for i in range(blocks):
        gs[i] = gram_ref[i // by, i % by]

    def put(stage):
        rows = pl.ds(stage * BASE, BASE)
        return pltpu.make_async_copy(fac_ref.at[:, :, rows], out_ref.at[:, :, rows], sem.at[stage])

    factor(gs, fac_ref, bx, by, order, put)
    for stage in range(order // BASE):
        put(stage).wait()
    fetch.wait()


def factor(gs, fac_ref, bx, by, order, put):
    blocks = bx * by
    lanes = lax.broadcasted_iota(jnp.int32, (order, order), 1)
    per = order // BASE
    seg = lax.broadcasted_iota(jnp.int32, (BASE, order), 1) // BASE
    place = lax.broadcasted_iota(jnp.int32, (BASE, order), 1) % BASE
    row = lax.broadcasted_iota(jnp.int32, (BASE, order), 0)
    seg8, place8, row8 = seg[:8], place[:8], row[:8]
    masks = [jnp.where(seg == q, 1.0, 0.0).astype(jnp.bfloat16) for q in range(per)]
    tops = BASE // 8
    groups = blocks // per
    for stage in range(per):
        low = stage * BASE
        high = low + BASE
        packs = []
        for g in range(groups):
            pack = None
            for q in range(per):
                piece = gs[g * per + q, low:high, :]
                shift = (q * BASE - low) % order
                piece = pltpu.roll(piece, shift, axis=1) if shift else piece
                pack = piece if pack is None else jnp.where(seg == q, piece, pack)
            packs.append([pack[8 * c:8 * c + 8] for c in range(tops)])
        pivots = [[jnp.ones((8, order), jnp.float32) for _ in range(tops)] for _ in range(groups)]
        for first in range(0, BASE, WIDTH):
            top = first // 8
            cols = [[[jnp.take_along_axis(m[c], seg8 * BASE + (first + j), axis=1) for c in range(top, tops)]
                     for j in range(WIDTH)] for m in packs]
            for j in range(WIDTH):
                k = first + j
                at = k - 8 * top
                for g, m in enumerate(packs):
                    f = cols[g][j]
                    d = jnp.broadcast_to(f[0][at:at + 1], (8, order))
                    inv_d = 1.0 / d
                    pivots[g][top] = jnp.where(row8 == at, d, pivots[g][top])
                    f = [jnp.where(row8 > at, f[0], 0.0)] + f[1:]
                    for n in range(j + 1, WIDTH):
                        t = jnp.broadcast_to(cols[g][n][0][at:at + 1], (8, order)) * inv_d
                        cols[g][n] = [x - y * t for x, y in zip(cols[g][n], f)]
                    r = (jnp.broadcast_to(m[top][at:at + 1], (8, order)) + jnp.where(place8 == k, 1.0, 0.0)) * inv_d
                    for c in range(top, tops):
                        m[c] = m[c] - f[c - top] * r
        for g, m in enumerate(packs):
            m = jnp.concatenate(m, axis=0)
            unit = jnp.where(row > place, m, jnp.where(row == place, 1.0, 0.0))
            inv = unit * lax.rsqrt(jnp.concatenate(pivots[g], axis=0))
            inv_h, inv_l = split(inv)
            wide_h = jnp.concatenate([inv_h * mask for mask in masks], axis=0)
            wide_l = jnp.concatenate([inv_l * mask for mask in masks], axis=0)
            panel = []
            for q in range(per):
                here = gs[g * per + q, low:high, :]
                panel.append(jnp.where(seg == stage, jnp.where(row == place, 1.0, 0.0), here))
            panel_h, panel_l = split(jnp.concatenate(panel, axis=0))
            whole = jnp.dot(jnp.concatenate([wide_h, wide_h, wide_l], axis=1),
                            jnp.concatenate([panel_h, panel_l, panel_h], axis=0),
                            preferred_element_type=jnp.float32)
            for q in range(per):
                at = g * per + q
                part = whole[q * BASE:(q + 1) * BASE]
                fac_ref[at // by, at % by, low:high, :] = jnp.where(seg <= stage, part, 0.0).astype(fac_ref.dtype)
                if high < order:
                    h, l = split(part)
                    left = jnp.concatenate([h, h, l], axis=0).T
                    update = jnp.dot(left[high:], jnp.concatenate([h, l, h], axis=0), preferred_element_type=jnp.float32)
                    below = gs[at, high:, :]
                    below = jnp.where(lanes[high:] // BASE == stage, 0.0, below)
                    gs[at, high:, :] = below - update
        put(stage).start()


def sum_kernel(fac_ref, v_ref, wt, out_ref, img, loc, px, py, rx, ry, send_sem, recv_sem):
    bx, by = fac_ref.shape[:2]
    there, exists = neighbours()
    gx_dirs, gy_dirs = DIRS[:2], DIRS[2:4]
    barrier = pltpu.get_barrier_semaphore()
    for d in DIRS[:4]:
        @pl.when(exists(d))
        def _(d=d):
            pl.semaphore_signal(barrier, inc=1, device_id=there(d), device_id_type=MESH)

    def remote(source, target, k, d):
        return pltpu.make_async_remote_copy(
            src_ref=source, dst_ref=target, send_sem=send_sem.at[k], recv_sem=recv_sem.at[k],
            device_id=there(d), device_id_type=MESH)

    def gx_copy(k, y):
        return remote(px.at[k, y], rx.at[k, y], k * by + y, gx_dirs[k])

    def gy_copy(k, x):
        return remote(py.at[k, x], ry.at[k, x], 2 * by + k * (bx + 2) + x, gy_dirs[k])

    def image(x, y):
        img[x, y] = lax.dot_general(fac_ref[x, y], v_ref[x, y], (((0,), (0,)), ((), ())),
                                    preferred_element_type=jnp.float32)

    def target(tx, ty):
        total = None
        for x in range(bx):
            for y in range(by):
                ax, ay = tx - x, ty - y
                if 0 <= ax < 3 and 0 <= ay < 3:
                    term = wt[ax * 3 + ay, x, pl.ds(y, 1), :] * img[x, y]
                    total = term if total is None else total + term
        return total

    rows = (bx + 1, 0)
    edges = (by - 1, 0)
    ends = sorted({0, by - 1})
    for y in ends:
        for x in range(bx):
            image(x, y)
    for k in range(2):
        for r in rows:
            py[k, r] = target(r, (by + 1, 0)[k]).astype(py.dtype)
    near = [exists(d).astype(jnp.int32) for d in DIRS[:4]]
    pl.semaphore_wait(barrier, near[0] + near[1] + near[2] + near[3])
    for k, d in enumerate(gy_dirs):
        @pl.when(exists(d))
        def _(k=k):
            for r in rows:
                gy_copy(k, r).start()

        @pl.when(jnp.logical_not(exists((-d[0], -d[1]))))
        def _(k=k):
            ry[k] = jnp.zeros(ry.shape[1:], ry.dtype)
    for k, d in enumerate(gx_dirs):
        @pl.when(jnp.logical_not(exists((-d[0], -d[1]))))
        def _(k=k):
            rx[k] = jnp.zeros(rx.shape[1:], rx.dtype)
    ready = set(ends)
    for y in range(1, by - 1):
        for n in (y - 1, y, y + 1):
            if n not in ready:
                ready.add(n)
                for x in range(bx):
                    image(x, n)
        for k, d in enumerate(gx_dirs):
            px[k, y] = target(rows[k], y + 1).astype(px.dtype)
        for k, d in enumerate(gx_dirs):
            @pl.when(exists(d))
            def _(k=k, y=y):
                gx_copy(k, y).start()
    for k in range(2):
        for x in range(1, bx + 1):
            py[k, x] = target(x, (by + 1, 0)[k]).astype(py.dtype)
    for k, d in enumerate(gy_dirs):
        @pl.when(exists(d))
        def _(k=k):
            for x in range(1, bx + 1):
                gy_copy(k, x).start()
    for y in ends:
        for x in range(bx):
            loc[x, y] = target(x + 1, y + 1)
    for k, d in enumerate(gy_dirs):
        @pl.when(exists((-d[0], -d[1])))
        def _(k=k):
            for r in rows:
                gy_copy(k, r).wait_recv()
    for y in ends:
        for k in range(2):
            total = target(rows[k], y + 1)
            for j in range(2):
                if y == edges[1 - j]:
                    total = total + ry[j, rows[k]].astype(jnp.float32)
            px[k, y] = total.astype(px.dtype)
        for k, d in enumerate(gx_dirs):
            @pl.when(exists(d))
            def _(k=k, y=y):
                gx_copy(k, y).start()
    for x in range(bx):
        for y in range(1, by - 1):
            loc[x, y] = target(x + 1, y + 1)
    for k, d in enumerate(gy_dirs):
        @pl.when(exists((-d[0], -d[1])))
        def _(k=k):
            for x in range(1, bx + 1):
                gy_copy(k, x).wait_recv()
    for y in list(range(1, by - 1)) + ends:
        for k, d in enumerate(gx_dirs):
            @pl.when(exists((-d[0], -d[1])))
            def _(k=k, y=y):
                gx_copy(k, y).wait_recv()
        for x in range(bx):
            total = loc[x, y]
            for k in range(2):
                if x == (0, bx - 1)[k]:
                    total = total + rx[k, y].astype(jnp.float32)
                if y == edges[1 - k]:
                    total = total + ry[k, x + 1].astype(jnp.float32)
            out_ref[x, y] = total.astype(out_ref.dtype)
    for k, d in enumerate(gx_dirs):
        @pl.when(exists(d))
        def _(k=k):
            for y in range(by):
                gx_copy(k, y).wait_send()
    for k, d in enumerate(gy_dirs):
        @pl.when(exists(d))
        def _(k=k):
            for x in range(bx + 2):
                gy_copy(k, x).wait_send()


def local(coeffs, permit, shift_diag, codes, counts, weights, vectors):
    bx, by, coupling, order = coeffs.shape
    nv = vectors.shape[3]
    bf16, f32 = jnp.bfloat16, jnp.float32
    anyspace = pl.BlockSpec(memory_space=pl.ANY)
    vmem = pl.BlockSpec(memory_space=pltpu.VMEM)
    codes, weights = jnp.transpose(codes, (2, 0, 1)), jnp.transpose(weights, (2, 0, 1))
    wide = by + 2
    packed = order // 2 + order // 8
    copies = 2 * bx + 2 + 2 * by
    gram, sums = pl.pallas_call(
        gram_kernel,
        out_shape=(pltpu.VMEM((bx, by, order, order), f32), pltpu.VMEM((9, bx, by, order), f32)),
        in_specs=[anyspace] * 6,
        out_specs=(vmem, vmem),
        scratch_shapes=[
            pltpu.VMEM((bx * wide, coupling, order), bf16),
            pltpu.VMEM((bx * wide, order, coupling), bf16),
            pltpu.VMEM(permit.shape, f32), pltpu.VMEM(shift_diag.shape, f32),
            pltpu.VMEM(codes.shape, jnp.int32), pltpu.VMEM(counts.shape, jnp.int32), pltpu.VMEM(weights.shape, f32),
            pltpu.VMEM((order, order), f32),
            pltpu.VMEM((bx, 9, by, coupling), f32),
            pltpu.VMEM((2, 3, by, coupling), bf16), pltpu.VMEM((2, 3, by, coupling), bf16),
            pltpu.VMEM((2, by, packed, order), f32), pltpu.VMEM((2, by, packed, order), f32),
            pltpu.SemaphoreType.DMA((bx,)), pltpu.SemaphoreType.DMA((5,)),
            pltpu.SemaphoreType.DMA((copies,)), pltpu.SemaphoreType.DMA((copies,)),
        ],
        compiler_params=pltpu.CompilerParams(collective_id=0, has_side_effects=True),
        name="gram",
    )(coeffs, permit, shift_diag, codes, counts, weights)
    fac, held, vecs = pl.pallas_call(
        factor_kernel,
        out_shape=(
            jax.ShapeDtypeStruct((bx, by, order, order), bf16),
            pltpu.VMEM((bx, by, order, order), bf16),
            pltpu.VMEM((bx, by, order, nv), bf16),
        ),
        in_specs=[vmem, anyspace],
        out_specs=(anyspace, vmem, vmem),
        scratch_shapes=[
            pltpu.VMEM((bx * by, order, order), f32), pltpu.SemaphoreType.DMA,
            pltpu.SemaphoreType.DMA((order // BASE,)),
        ],
        name="factor",
    )(pltpu.with_memory_space_constraint(gram, pltpu.VMEM), vectors)
    edges = [pltpu.VMEM((2, by, order, nv), bf16), pltpu.VMEM((2, bx + 2, order, nv), bf16)]
    copies = 2 * by + 2 * (bx + 2)
    applied = pl.pallas_call(
        sum_kernel,
        out_shape=pltpu.VMEM((bx, by, order, nv), bf16),
        in_specs=[vmem, vmem, vmem],
        out_specs=vmem,
        scratch_shapes=[
            pltpu.VMEM((bx, by, order, nv), f32),
            pltpu.VMEM((bx, by, order, nv), f32),
            *edges, *edges,
            pltpu.SemaphoreType.DMA((copies,)), pltpu.SemaphoreType.DMA((copies,)),
        ],
        compiler_params=pltpu.CompilerParams(collective_id=1, has_side_effects=True),
        name="sums",
    )(*(pltpu.with_memory_space_constraint(x, pltpu.VMEM) for x in (held, vecs, sums)))
    return fac, applied


def solution(mesh):
    placed = (
        P("gx", "gy", None, None),
        P("gx", "gy", None),
        P("gx", "gy", None),
        P("gx", "gy", None),
        P("gx", "gy"),
        P("gx", "gy", None),
        P("gx", "gy", None, None),
    )
    return jax.shard_map(
        local,
        mesh=mesh,
        in_specs=placed,
        out_specs=(P("gx", "gy", None, None), P("gx", "gy", None, None)),
        check_vma=False,
    )
```
